256 devices in a mesh: depth: 64 (over z, y, core), tile: 4 (over x).
Axes of the slice: x: 4, y: 4, z: 8, core: 2. Of those that a mesh axis runs over, the one named last changes fastest.
Arguments:
- volume: bfloat16 [768, 4, 768, 512], P('depth', 'tile'), may hold values from -6 to 6
- table_index: int32 [768, 4, 768, 32], P('depth', 'tile'), may hold values from 0 to 15
- brick_position: int32 [64], replicated, may hold values from 0 to 63, each once
- tf_center: float32 [16], replicated, may hold values from -1.5 to 1.5
- tf_width: float32 [16], replicated, may hold values from 0.3 to 1.2
- tf_peak: float32 [16], replicated, may hold values from 2 to 32
- tf_color: float32 [3, 16], replicated, may hold values from 0.1 to 1
Outputs:
- frame: float32 [4, 4, 768, 512], P(None, 'tile', 'depth')
The draws below stay inside these ranges and needn't reach their ends.
Inputs may be any that keep to these rules, and one draw needn't show every extreme that they name: `brick_position`: each depth rank has a different position.
All inputs are finite; a program needn't handle non-finite values.
Results may differ from the reference program's by a relative error of at most 0.0003.
Values may be sent and summed in bfloat16 or wider, within the bound.
No kernel may reach another device: no remote copies, remote signals or barrier semaphores. Data moves between devices by JAX's collectives and lax.ppermute only.
A program may use at most 128 MiB of HBM per device.

```python
import math
import jax
import jax.numpy as jnp
from jax import lax

SLAB = 12
TH = 768
TW = 512
TABLE = 16
CELL = 16
NZ = 768
CELLS = 32
N_DEPTH = 64
N_TILE = 4


def place_ends(entries, stream_key, low, largest):
    longest = entries.shape.index(max(entries.shape))
    spots = []
    for shift in (0, 1):
        where = [jax.random.randint(jax.random.fold_in(stream_key, axis), (), 0, length) for axis, length in enumerate(entries.shape)]
        where[longest] = (where[longest] + shift) % entries.shape[longest]
        spots.append(tuple(where))
    return entries.at[spots[0]].set(low).at[spots[1]].set(largest)


def shard_levels(stream_key, extent, split, low, high):
    factor_of = 1.0
    for dim, blocks in split:
        steps = jax.random.uniform(jax.random.fold_in(jax.random.fold_in(stream_key, 6), dim), (blocks,), jnp.float32, low / len(split), high / len(split))
        factor_of = factor_of * jnp.repeat(jnp.exp(steps), extent[dim] // blocks).reshape((-1,) + (1,) * (len(extent) - 1 - dim))
    return factor_of


def normal_values(stream_key, dims, deviation, reach, cuts=(), kind=jnp.bfloat16):
    values = jax.random.normal(stream_key, dims, jnp.float32) * deviation
    if len(cuts) > 0:
        values = shard_levels(stream_key, dims, cuts, -0.22, 0.18) * values
    return jnp.clip(values, min=-reach, max=reach).astype(kind)


def setup_inputs(seed: int = 0) -> dict:
    seeds = jax.random.split(jax.random.key(seed), 8)
    return {
        "volume": normal_values(seeds[0], (NZ, N_TILE, TH, TW), 1.0, 6.0, ((0, 64), (1, 4))),
        "table_index": place_ends(jax.random.randint(seeds[1], (NZ, N_TILE, TH, CELLS), 0, TABLE), jax.random.fold_in(seeds[1], 1), 0, TABLE - 1).astype(jnp.int32),
        "brick_position": jax.random.permutation(seeds[2], N_DEPTH).astype(jnp.int32),
        "tf_center": jnp.clip(jax.random.uniform(seeds[3], (TABLE,), jnp.float32, -1.5, 1.5), -1.5, 1.5),
        "tf_width": jnp.clip(jnp.exp(jax.random.uniform(seeds[4], (TABLE,), jnp.float32, math.log(0.3), math.log(1.2))), 0.3, 1.2),
        "tf_peak": jnp.clip(jnp.exp(jax.random.uniform(seeds[5], (TABLE,), jnp.float32, math.log(2.0), math.log(32.0))), 2.0, 32.0),
        "tf_color": jnp.clip(jax.random.uniform(seeds[6], (3, TABLE), jnp.float32, 0.1, 1.0), 0.1, 1.0),
    }


def light_sample(value, grad_x, grad_y, params, rgb, trans, inverse):
    energy = grad_x * grad_x + grad_y * grad_y
    facing = 0.6 * grad_x + 0.8 * grad_y
    shade = 0.3 + 0.7 * facing * facing / (1.0 + energy)
    scaled = (value - params[0]) / params[1]
    extinction = params[2] * jnp.exp(-0.5 * scaled * scaled) * energy * inverse
    keep = jnp.exp(-extinction)
    opacity = 1.0 - keep
    weight = trans * opacity
    rgb = rgb + weight[None] * params[3:6] * shade[None]
    trans = trans * keep
    return rgb, trans


def to_plane(block):
    shape = block.shape
    block = block.reshape(shape[0], 2, 2, shape[2], shape[3])
    return block.transpose(0, 1, 3, 2, 4).reshape(shape[0], 2 * shape[2], 2 * shape[3])


def march(padded, cells, tables):
    height = cells.shape[1]
    width = cells.shape[2]
    inverse = 1.0 / NZ

    def sample(step, carry):
        rgb, trans = carry
        plane = lax.dynamic_index_in_dim(padded, step, 0, keepdims=False)
        index = lax.dynamic_index_in_dim(cells, step, 0, keepdims=False)
        value = plane[1:-1, 1:-1]
        grad_x = 0.5 * (plane[1:-1, 2:] - plane[1:-1, :-2])
        grad_y = 0.5 * (plane[2:, 1:-1] - plane[:-2, 1:-1])
        params = jnp.take(tables, index, axis=1)
        return light_sample(value, grad_x, grad_y, params, rgb, trans, inverse)

    start = (jnp.zeros((3, height, width), jnp.float32), jnp.ones((height, width), jnp.float32))
    rgb, trans = lax.fori_loop(0, SLAB, sample, start)
    return jnp.concatenate([rgb, (1.0 - trans)[None]], axis=0)


def reference(volume, table_index, brick_position, tf_center, tf_width, tf_peak, tf_color):
    tables = jnp.concatenate([tf_center[None], tf_width[None], tf_peak[None], tf_color], axis=0).astype(jnp.float32)
    rank_at = jnp.argsort(brick_position).astype(jnp.int32)

    def step(image, place):
        rank = rank_at[place]
        brick = lax.dynamic_slice_in_dim(volume, rank * SLAB, SLAB, 0)
        cells = lax.dynamic_slice_in_dim(table_index, rank * SLAB, SLAB, 0)
        plane = to_plane(brick.astype(jnp.float32))
        index = to_plane(jnp.repeat(cells, CELL, axis=3))
        padded = jnp.pad(plane, ((0, 0), (1, 1), (1, 1)))
        partial_value = march(padded, index, tables)
        return image + (1.0 - image[3:4]) * partial_value, None

    start = jnp.zeros((4, 2 * TH, 2 * TW), jnp.float32)
    image, unused = lax.scan(step, start, jnp.arange(N_DEPTH, dtype=jnp.int32))
    image = image.reshape(4, 2, TH, 2, TW).transpose(0, 1, 3, 2, 4)
    return image.reshape(4, 4, TH, TW)
```

```python
import functools

import jax
import jax.numpy as jnp
from jax import lax
from jax.experimental import pallas as pl
from jax.experimental.pallas import tpu as pltpu
from jax.sharding import PartitionSpec as P

CELL = 16
LANES = 128
SIDE = 8
BAND = 256
LOG2E = 1.4426950408889634
LEVELS = 65535.0
CHUNKS = ((1,), (0, 2, 3))
STEP_SAMPLES = 3

NT = (((1,), (1,)), ((), ()))
NN = (((1,), (0,)), ((), ()))


def from_partner(value, axis, apart):
    return lax.ppermute(value, axis, [(i, i ^ 1 << apart) for i in range(lax.axis_size(axis))])


def tile_of(tiles, j):
    tile = jnp.int32(tiles[0])
    for n in range(1, len(tiles)):
        tile = jnp.where(j == n, jnp.int32(tiles[n]), tile)
    return tile


def code(value):
    root = lax.rsqrt(lax.rsqrt(jnp.maximum(value, 0.0)))
    return jnp.minimum(root * LEVELS + 0.5, LEVELS).astype(jnp.int32)


def decode(word):
    root = word.astype(jnp.float32) * (1.0 / LEVELS)
    square = root * root
    return square * square


def march_kernel(tiles, sizes, *refs):
    steps, height, width, total = sizes
    (center_ref, wide_ref, peak_ref, color_ref, vol_ref, rim_row_ref, index_ref, rim_col_ref) = refs[:8]
    if rim_col_ref is None:
        out_ref, edge_ref = refs[8:10]
        scratch = refs[10:]
    else:
        out_ref = refs[8]
        edge_ref = None
        scratch = refs[9:]
    (pick_ref, band_ref, ends_ref, table_ref, value_ref, grad_ref, param_ref, pair_a, pair_b, turn_a, turn_b) = scratch
    j = pl.program_id(0)
    part = pl.program_id(1)
    tile = tile_of(tiles, j)
    span = LANES + 2 * SIDE

    @pl.when(part == 0)
    def _():
        row = lax.broadcasted_iota(jnp.int32, (span, width), 0)
        col = lax.broadcasted_iota(jnp.int32, (span, width), 1)
        want = tile * LANES + row - SIDE
        want = jnp.where(row == 0, 0, jnp.where(row == 1, width - 1, want))
        pick_ref[...] = jnp.where(col == want, 1.0, 0.0).astype(jnp.bfloat16)

    @pl.when((part == 0) & (j == 0))
    def _():
        k = lax.broadcasted_iota(jnp.int32, (BAND, BAND), 0)
        r = lax.broadcasted_iota(jnp.int32, (BAND, BAND), 1)
        band = jnp.where(k == r + 1, 1.0, jnp.where(k == r - 1, -1.0, 0.0))
        band_ref[...] = band.astype(jnp.bfloat16)
        k = lax.broadcasted_iota(jnp.int32, (16, BAND), 0)
        r = lax.broadcasted_iota(jnp.int32, (16, BAND), 1)
        for n in range(height // BAND):
            above = (k == 2 * n) & (r == 0)
            below = (k == 2 * n + 1) & (r == BAND - 1)
            ends_ref[n] = jnp.where(below, 1.0, jnp.where(above, -1.0, 0.0)).astype(jnp.bfloat16)
        shape = (8, 16)
        scale = (0.5 * LOG2E) ** 0.5 / wide_ref[...]
        table_ref[0, :, 0:16] = jnp.broadcast_to(center_ref[...], shape)
        table_ref[1, :, 0:16] = jnp.broadcast_to(scale, shape)
        table_ref[2, :, 0:16] = jnp.broadcast_to(jnp.log2(peak_ref[...] * (0.25 * LOG2E / total)), shape)
        for n in range(3):
            table_ref[3 + n, :, 0:16] = jnp.broadcast_to(color_ref[n : n + 1, :], shape)

    pick = pick_ref[...]
    inner = pick[SIDE : SIDE + LANES]
    for q in range(STEP_SAMPLES):
        s = part * STEP_SAMPLES + q
        rims = lax.dot_general(inner, rim_row_ref[q], NT, preferred_element_type=jnp.float32).astype(jnp.bfloat16)
        for n in range(height // BAND):
            rows = slice(BAND * n, BAND * n + BAND)
            turned = lax.dot_general(pick, vol_ref[q, rows, :], NT, preferred_element_type=jnp.float32)
            for m in range(BAND // LANES):
                value_ref[s, 2 * n + m] = turned[:, LANES * m : LANES * m + LANES]
            short = turned[SIDE : SIDE + LANES].astype(jnp.bfloat16)
            grad = lax.dot_general(short, band_ref[...], NN, preferred_element_type=jnp.float32)
            grad = grad + lax.dot_general(rims, ends_ref[n], NN, preferred_element_type=jnp.float32)
            for m in range(BAND // LANES):
                grad_ref[s, 2 * n + m] = grad[:, LANES * m : LANES * m + LANES]
        if edge_ref is not None:
            for n in range(height // LANES):
                edge_ref[q, :, LANES * n : LANES * n + LANES] = value_ref[s, n, 0:SIDE, :]
        if rim_col_ref is not None:

            @pl.when(tile == 0)
            def _():
                for n in range(height // LANES):
                    value_ref[s, n, SIDE - 1 : SIDE, :] = rim_col_ref[q, 0:1, LANES * n : LANES * n + LANES]

            @pl.when(tile == width // LANES - 1)
            def _():
                for n in range(height // LANES):
                    value_ref[s, n, SIDE + LANES : SIDE + LANES + 1, :] = rim_col_ref[q, 1:2, LANES * n : LANES * n + LANES]

        for n in range(height // LANES):
            lanes = slice(LANES * n, LANES * n + LANES)
            index = index_ref[q, :, lanes]
            for p in range(6):
                param_ref[s, p, n] = jnp.take_along_axis(table_ref[p], index, axis=1)

    @pl.when(part == steps // STEP_SAMPLES - 1)
    def _():
        groups = LANES // CELL

        def strip(i, carry):
            g = i % groups
            lane = i // groups
            base = pl.multiple_of(g * CELL, CELL)
            zero = jnp.zeros((8, LANES), jnp.float32)
            state = [[zero, zero + 1.0, zero, zero, zero] for _ in range(2)]
            for s in range(steps):
                param = [param_ref[s, p, lane, pl.ds(g, 8, stride=0), :] for p in range(6)]
                for u in range(2):
                    depth, trans, red, green, blue = state[u]
                    at = base + 8 * u
                    value = value_ref[s, lane, pl.ds(at + SIDE, 8), :]
                    ahead = value_ref[s, lane, pl.ds(at + SIDE + 1, 8), :]
                    behind = value_ref[s, lane, pl.ds(at + SIDE - 1, 8), :]
                    grad_x = ahead - behind
                    grad_y = grad_ref[s, lane, pl.ds(at, 8), :]
                    energy = grad_x * grad_x + grad_y * grad_y
                    facing = 0.6 * grad_x + 0.8 * grad_y
                    shade = 0.3 + 0.7 * (facing * facing / (4.0 + energy))
                    scaled = (value - param[0]) * param[1]
                    rate = jnp.exp2(param[2] - scaled * scaled)
                    depth = depth - rate * energy
                    after = jnp.exp2(depth)
                    weight = (trans - after) * shade
                    red = red + weight * param[3]
                    green = green + weight * param[4]
                    blue = blue + weight * param[5]
                    state[u] = [depth, after, red, green, blue]
            for u in range(2):
                depth, trans, red, green, blue = state[u]
                at = pl.ds(base + 8 * u, 8)
                pair_a[lane, at, :] = (code(red) << 16) | code(green)
                pair_b[lane, at, :] = (code(blue) << 16) | code(1.0 - trans)
            return carry

        lax.fori_loop(0, groups * (height // LANES), strip, 0)
        for n in range(height // LANES):
            lanes = slice(LANES * n, LANES * n + LANES)
            turn_a[lanes, :] = pair_a[n].T
            turn_b[lanes, :] = pair_b[n].T

        def pack(d, carry):
            for u in range(4):
                e = d * 4 + u
                r = e * 12
                out_ref[e, 0:8, :] = turn_a[pl.ds(r, 8), :]
                out_ref[e, 8:12, :] = turn_a[pl.ds(r + 8, 4), :]
                out_ref[e, 12:16, :] = turn_b[pl.ds(r + 8, 4), :]
                out_ref[e, 16:24, :] = turn_b[pl.ds(r, 8), :]
            return carry

        lax.fori_loop(0, out_ref.shape[0] // 4, pack, 0)


def march(tiles, ranks, tables, samples, rim_rows, cells, rim_cols):
    steps, height, width = samples.shape
    ahead = rim_cols is None
    span = LANES + 2 * SIDE
    batch = STEP_SAMPLES
    sizes = (steps, height, width, steps * ranks)

    def body(*refs):
        refs = list(refs)
        if ahead:
            refs.insert(7, None)
        march_kernel(tiles, sizes, *refs)

    small = lambda shape: pl.BlockSpec(shape, lambda j, s: (0, 0))
    in_specs = [small((1, 16)), small((1, 16)), small((1, 16)), small((3, 16))]
    in_specs += [
        pl.BlockSpec((batch, height, width), lambda j, s: (s, 0, 0)),
        pl.BlockSpec((batch, 16, width), lambda j, s: (s, 0, 0)),
        pl.BlockSpec((batch, LANES // CELL, height), lambda j, s: (s, tile_of(tiles, j), 0)),
    ]
    piece = height // ranks
    out_shape = [jax.ShapeDtypeStruct((ranks, 2 * piece, LANES * len(tiles)), jnp.int32)]
    out_specs = [pl.BlockSpec((ranks, 2 * piece, LANES), lambda j, s: (0, 0, j))]
    args = list(tables) + [samples, rim_rows, cells]
    if ahead:
        out_shape.append(jax.ShapeDtypeStruct((steps, SIDE, height), jnp.float32))
        out_specs.append(pl.BlockSpec((batch, SIDE, height), lambda j, s: (s, 0, 0)))
    else:
        in_specs.append(pl.BlockSpec((batch, 2, height), lambda j, s: (s, 0, 0)))
        args.append(rim_cols)
    points = steps * height * LANES * len(tiles)
    return pl.pallas_call(
        body,
        grid=(len(tiles), steps // batch),
        in_specs=in_specs,
        out_specs=out_specs,
        out_shape=out_shape,
        scratch_shapes=[
            pltpu.VMEM((span, width), jnp.bfloat16),
            pltpu.VMEM((BAND, BAND), jnp.bfloat16),
            pltpu.VMEM((height // BAND, 16, BAND), jnp.bfloat16),
            pltpu.VMEM((6, 8, LANES), jnp.float32),
            pltpu.VMEM((steps, height // LANES, span, LANES), jnp.float32),
            pltpu.VMEM((steps, height // LANES, LANES, LANES), jnp.float32),
            pltpu.VMEM((steps, 6, height // LANES, LANES // CELL, LANES), jnp.float32),
            pltpu.VMEM((height // LANES, LANES, LANES), jnp.int32),
            pltpu.VMEM((height // LANES, LANES, LANES), jnp.int32),
            pltpu.VMEM((height, LANES), jnp.int32),
            pltpu.VMEM((height, LANES), jnp.int32),
        ],
        compiler_params=pltpu.CompilerParams(
            dimension_semantics=("arbitrary", "arbitrary"), vmem_limit_bytes=56 * 1024 * 1024
        ),
        cost_estimate=pl.CostEstimate(flops=40 * points, bytes_accessed=2 * points, transcendentals=3 * points),
        name="march",
    )(*args)


def blend_kernel(tiles, place_ref, got_ref, *refs):
    out_ref, rank_ref = refs[-2:]
    ranks = got_ref.shape[0]

    def note(d, carry):
        rank_ref[place_ref[d]] = d
        return carry

    lax.fori_loop(0, ranks, note, 0)
    count = len(tiles)
    lower = lax.broadcasted_iota(jnp.int32, (8, LANES), 0) < 4
    zero = jnp.zeros((8, LANES), jnp.float32)
    one = zero + 1.0

    def layer(i, carry):
        carry = list(carry)
        for u in range(2):
            d = rank_ref[i * 2 + u]
            for n in range(count):
                lanes = slice(LANES * n, LANES * n + LANES)
                red, green, blue, alpha, trans, high, low, half = carry[n]
                first = got_ref[d, 0:8, lanes]
                mixed = got_ref[d, 8:16, lanes]
                last = got_ref[d, 16:24, lanes]
                cover = decode(last & 0xFFFF) * trans
                red = red + trans * decode(lax.shift_right_logical(first, 16))
                green = green + trans * decode(first & 0xFFFF)
                blue = blue + trans * decode(lax.shift_right_logical(last, 16))
                alpha = alpha + cover
                trans = trans - cover
                level = decode(mixed & 0xFFFF)
                opaque = jnp.where(lower, pltpu.roll(level, 4, 0), level)
                high = high + half * decode(lax.shift_right_logical(mixed, 16))
                low = low + half * level
                half = half - half * opaque
                carry[n] = (red, green, blue, alpha, trans, high, low, half)
        return tuple(carry)

    start = tuple((zero, zero, zero, zero, one, zero, zero, one) for _ in range(count))
    final = lax.fori_loop(0, ranks // 2, layer, start)
    for n in range(count):
        lanes = slice(LANES * tiles[n], LANES * tiles[n] + LANES)
        red, green, blue, alpha, trans, high, low, half = final[n]
        out_ref[0, 0:8, lanes] = red
        out_ref[1, 0:8, lanes] = green
        out_ref[2, 0:8, lanes] = blue
        out_ref[3, 0:8, lanes] = alpha
        out_ref[0, 8:12, lanes] = high[0:4]
        out_ref[1, 8:12, lanes] = low[0:4]
        out_ref[2, 8:12, lanes] = high[4:8]
        out_ref[3, 8:12, lanes] = low[4:8]


def blend(tiles, brick_position, got, image, width):
    ranks, rows, lanes = got.shape
    piece = rows // 2
    whole = pl.BlockSpec(memory_space=pltpu.VMEM)
    in_specs = [pl.BlockSpec(memory_space=pltpu.SMEM), whole]
    args = [brick_position, got]
    body = functools.partial(blend_kernel, tiles)
    if image is not None:
        inner = body

        def body(place_ref, got_ref, image_ref, out_ref, rank_ref):
            out_ref[...] = image_ref[...]
            inner(place_ref, got_ref, out_ref, rank_ref)

        in_specs.append(whole)
        args.append(image)
    return pl.pallas_call(
        body,
        in_specs=in_specs,
        out_specs=whole,
        out_shape=jax.ShapeDtypeStruct((4, piece, width), jnp.float32),
        scratch_shapes=[pltpu.SMEM((ranks,), jnp.int32)],
        cost_estimate=pl.CostEstimate(flops=40 * got.size, bytes_accessed=4 * got.size, transcendentals=0),
        name="blend",
    )(*args)


def on_device(volume, table_index, brick_position, tf_center, tf_width, tf_peak, tf_color):
    samples = volume[:, 0]
    cells = jnp.swapaxes(table_index[:, 0], 1, 2)
    height = samples.shape[1]
    width = samples.shape[2]
    ranks = lax.axis_size("depth")
    tables = [tf_center[None], tf_width[None], tf_peak[None], tf_color]
    tile_rank = lax.axis_index("tile")
    col_bit = tile_rank % 2
    row_bit = tile_rank // 2
    send_row = jnp.where(row_bit == 0, samples[:, height - 1, :], samples[:, 0, :])
    got_row = from_partner(send_row, "tile", 1)
    zero_row = jnp.zeros_like(got_row)
    ends = [jnp.where(row_bit == 1, got_row, zero_row)]
    for n in range(1, height // BAND):
        ends += [samples[:, BAND * n, :], samples[:, BAND * n - 1, :]]
    ends += [jnp.where(row_bit == 0, got_row, zero_row)]
    rim_rows = jnp.stack(ends, axis=1)
    rim_rows = jnp.pad(rim_rows, ((0, 0), (0, 16 - len(ends)), (0, 0)))
    early, edges = march(CHUNKS[0], ranks, tables, samples, rim_rows, cells, None)
    swap = functools.partial(lax.all_to_all, axis_name="depth", split_axis=0, concat_axis=0, tiled=True)
    got_early = swap(early)
    send_col = jnp.where(col_bit == 0, edges[:, 1], edges[:, 0]).astype(jnp.bfloat16)
    got_col = from_partner(send_col, "tile", 0).astype(jnp.float32)
    zero_col = jnp.zeros_like(got_col)
    rim_cols = jnp.stack([jnp.where(col_bit == 1, got_col, zero_col), jnp.where(col_bit == 0, got_col, zero_col)], axis=1)
    (late,) = march(CHUNKS[1], ranks, tables, samples, rim_rows, cells, rim_cols)
    got_late = swap(late)
    image = blend(CHUNKS[0], brick_position, got_early, None, width)
    image = blend(CHUNKS[1], brick_position, got_late, image, width)
    return image[:, None]


def solution(mesh):
    return jax.shard_map(
        on_device,
        mesh=mesh,
        in_specs=(
            P("depth", "tile", None, None),
            P("depth", "tile", None, None),
            P(),
            P(),
            P(),
            P(),
            P(),
        ),
        out_specs=P(None, "tile", "depth", None),
        check_vma=False,
    )
```

```python
import functools

import jax
import jax.numpy as jnp
from jax import lax
from jax.experimental import pallas as pl
from jax.experimental.pallas import tpu as pltpu
from jax.sharding import PartitionSpec as P

CELL = 16
LANES = 128
SIDE = 8
BAND = 256
LOG2E = 1.4426950408889634
LEVELS = 65535.0
CHUNKS = ((1, 2), (0, 3))
EDGES = 8
SHADE_GAIN = 0.7 * 0.6 * 0.6
SHADE_BASE = 0.3 / SHADE_GAIN

NT = (((1,), (1,)), ((), ()))
NN = (((1,), (0,)), ((), ()))


def from_partner(value, axis, apart):
    return lax.ppermute(value, axis, [(i, i ^ 1 << apart) for i in range(lax.axis_size(axis))])


def tile_of(tiles, j):
    tile = jnp.int32(tiles[0])
    for n in range(1, len(tiles)):
        tile = jnp.where(j == n, jnp.int32(tiles[n]), tile)
    return tile


def code(value):
    root = lax.rsqrt(lax.rsqrt(jnp.maximum(value, 0.0)))
    return jnp.minimum(root * LEVELS + 0.5, LEVELS).astype(jnp.int32)


def decode(word):
    root = word.astype(jnp.float32) * (1.0 / LEVELS)
    square = root * root
    return square * square


def march_kernel(tiles, sizes, *refs):
    steps, height, width, total = sizes
    count = len(tiles)
    center_ref, wide_ref, peak_ref, color_ref, vol_ref, rim_ref, index_ref, halo_ref = refs[:8]
    if halo_ref is None:
        out_ref, edge_ref = refs[8:10]
        scratch = refs[10:]
    else:
        out_ref = refs[8]
        edge_ref = None
        scratch = refs[9:]
    (band_ref, table_ref, left_ref, value_ref, grad_ref, param_ref, pair_a, pair_b, turn_a, turn_b) = scratch[:10]
    part = pl.program_id(0)
    halves = BAND // LANES
    groups = LANES // CELL

    @pl.when(part == 0)
    def _():
        k = lax.broadcasted_iota(jnp.int32, (BAND + LANES, BAND), 0)
        r = lax.broadcasted_iota(jnp.int32, (BAND + LANES, BAND), 1)
        rim = k >= BAND
        above = (~rim & (k == r - 1)) | (rim & (k % 2 == 0) & (r == 0))
        below = (~rim & (k == r + 1)) | (rim & (k % 2 == 1) & (r == BAND - 1))
        band_ref[...] = jnp.where(below, 1.0, jnp.where(above, -1.0, 0.0)).astype(jnp.bfloat16)
        shape = (8, 16)
        scale = (0.5 * LOG2E) ** 0.5 / wide_ref[...]
        table_ref[0, :, 0:16] = jnp.broadcast_to(center_ref[...], shape)
        table_ref[1, :, 0:16] = jnp.broadcast_to(scale, shape)
        table_ref[2, :, 0:16] = jnp.broadcast_to(jnp.log2(peak_ref[...] * (0.25 * LOG2E / total)), shape)
        for n in range(3):
            table_ref[3 + n, :, 0:16] = jnp.broadcast_to(color_ref[n : n + 1, :] * SHADE_GAIN, shape)
        if edge_ref is not None:
            spots_ref = scratch[10]
            col = lax.broadcasted_iota(jnp.int32, (width, LANES), 0)
            lane = lax.broadcasted_iota(jnp.int32, (width, LANES), 1)
            which = lane % EDGES
            want = jnp.where(which == 0, 0, (which + 1) // 2 * LANES - which % 2)
            for s in range(steps):
                hit = (col == want) & (lane // EDGES == s)
                spots_ref[s] = jnp.where(hit, 1.0, 0.0).astype(jnp.bfloat16)

    if edge_ref is not None:
        spots_ref = scratch[10]
        found = jnp.zeros((BAND, LANES), jnp.float32)
        for s in range(steps):
            found = found + lax.dot_general(vol_ref[s], spots_ref[s], NN, preferred_element_type=jnp.float32)
        edge_ref[...] = found.T

    pair_lane = lax.broadcasted_iota(jnp.int32, (LANES, LANES), 1) // 2
    rims = [rim_ref[:, LANES * t : LANES * t + LANES].astype(jnp.float32).T for t in tiles]
    batch = 3
    for q in range(steps // batch):
        for s in range(batch * q, batch * q + batch):
            for k in range(count):
                t = tiles[k]
                at = slice((s * count + k) * LANES, (s * count + k) * LANES + LANES)
                if edge_ref is None:
                    source = vol_ref[k][s]
                else:
                    source = vol_ref[s, :, LANES * t : LANES * t + LANES]
                turned = source.T
                left_ref[at, 0:BAND] = turned
                left_ref[at, BAND : BAND + LANES] = jnp.where(pair_lane == s, rims[k], 0.0).astype(jnp.bfloat16)
                for m in range(halves):
                    lanes = slice(LANES * m, LANES * m + LANES)
                    value_ref[s, k, m, SIDE : SIDE + LANES, :] = turned[:, lanes].astype(jnp.float32)
                    if edge_ref is None:
                        before = halo_ref[4 * s + 2 * k : 4 * s + 2 * k + 1, lanes]
                        after = halo_ref[4 * s + 2 * k + 1 : 4 * s + 2 * k + 2, lanes]
                    else:
                        before = edge_ref[EDGES * s + 2 * t - 1 : EDGES * s + 2 * t, lanes]
                        after = edge_ref[EDGES * s + 2 * t + 2 : EDGES * s + 2 * t + 3, lanes]
                    value_ref[s, k, m, SIDE - 1 : SIDE, :] = before
                    value_ref[s, k, m, SIDE + LANES : SIDE + LANES + 1, :] = after
                    index = index_ref[s, groups * t : groups * t + groups, lanes]
                    for p in range(6):
                        param_ref[s, p, k * halves + m] = jnp.take_along_axis(table_ref[p], index, axis=1)
        size = batch * count * LANES
        grad = lax.dot_general(left_ref[q * size : q * size + size, :], band_ref[...], NN, preferred_element_type=jnp.float32)
        for s in range(batch):
            for k in range(count):
                for m in range(halves):
                    at = (s * count + k) * LANES
                    grad_ref[q * batch + s, k * halves + m] = grad[at : at + LANES, LANES * m : LANES * m + LANES]

    def strip(i, carry):
        g = i % groups
        lane = i // groups
        k = lane // halves
        m = lane % halves
        base = pl.multiple_of(g * CELL, CELL)
        zero = jnp.zeros((8, LANES), jnp.float32)
        state = [[zero, zero + 1.0, zero, zero, zero] for _ in range(2)]
        for s in range(steps):
            param = [param_ref[s, p, lane, pl.ds(g, 8, stride=0), :] for p in range(6)]
            for u in range(2):
                depth, trans, red, green, blue = state[u]
                at = base + 8 * u
                value = value_ref[s, k, m, pl.ds(at + SIDE, 8), :]
                ahead = value_ref[s, k, m, pl.ds(at + SIDE + 1, 8), :]
                behind = value_ref[s, k, m, pl.ds(at + SIDE - 1, 8), :]
                grad_x = ahead - behind
                grad_y = grad_ref[s, lane, pl.ds(at, 8), :]
                energy = grad_x * grad_x + grad_y * grad_y
                facing = grad_x + (0.8 / 0.6) * grad_y
                shade = SHADE_BASE + facing * facing / (4.0 + energy)
                scaled = (value - param[0]) * param[1]
                rate = jnp.exp2(param[2] - scaled * scaled)
                depth = depth - rate * energy
                after = jnp.exp2(depth)
                weight = (trans - after) * shade
                red = red + weight * param[3]
                green = green + weight * param[4]
                blue = blue + weight * param[5]
                state[u] = [depth, after, red, green, blue]
        for u in range(2):
            depth, trans, red, green, blue = state[u]
            at = pl.ds(base + 8 * u, 8)
            pair_a[lane, at, :] = (code(red) << 16) | code(green)
            pair_b[lane, at, :] = (code(blue) << 16) | code(1.0 - trans)
        return carry

    lax.fori_loop(0, groups * count * halves, strip, 0)
    for k in range(count):
        for m in range(halves):
            rows = pl.ds(pl.multiple_of(part * BAND + m * LANES, LANES), LANES)
            turn_a[k, rows, :] = pair_a[k * halves + m].T
            turn_b[k, rows, :] = pair_b[k * halves + m].T

    @pl.when(part == height // BAND - 1)
    def _():
        piece = height // out_ref.shape[0]

        def pack(d, carry):
            for u in range(4):
                e = d * 4 + u
                r = e * piece
                for k in range(count):
                    lanes = slice(LANES * k, LANES * k + LANES)
                    out_ref[e, 0:8, lanes] = turn_a[k, pl.ds(r, 8), :]
                    out_ref[e, 8:12, lanes] = turn_a[k, pl.ds(r + 8, 4), :]
                    out_ref[e, 12:16, lanes] = turn_b[k, pl.ds(r + 8, 4), :]
                    out_ref[e, 16:24, lanes] = turn_b[k, pl.ds(r, 8), :]
            return carry

        lax.fori_loop(0, out_ref.shape[0] // 4, pack, 0)


def march(tiles, ranks, tables, samples, rim_rows, cells, halo):
    steps, height, width = samples.shape
    first = halo is None
    count = len(tiles)
    sizes = (steps, height, width, steps * ranks)
    halves = BAND // LANES

    def body(*refs):
        refs = list(refs)
        if first:
            refs.insert(7, None)
        else:
            refs[4 : 4 + count] = [refs[4 : 4 + count]]
        march_kernel(tiles, sizes, *refs)

    small = lambda shape: pl.BlockSpec(shape, lambda n: (0, 0))
    in_specs = [small((1, 16)), small((1, 16)), small((1, 16)), small((3, 16))]
    args = list(tables)
    if first:
        in_specs.append(pl.BlockSpec((steps, BAND, width), lambda n: (0, n, 0)))
        args.append(samples)
    else:
        for t in tiles:
            in_specs.append(pl.BlockSpec((steps, BAND, LANES), lambda n, t=t: (0, n, t)))
            args.append(samples)
    in_specs += [
        pl.BlockSpec((None, LANES, width), lambda n: (n, 0, 0)),
        pl.BlockSpec((steps, width // CELL, BAND), lambda n: (0, 0, n)),
    ]
    args += [rim_rows, cells]
    piece = height // ranks
    out_shape = [jax.ShapeDtypeStruct((ranks, 2 * piece, LANES * count), jnp.int32)]
    out_specs = [pl.BlockSpec((ranks, 2 * piece, LANES * count), lambda n: (0, 0, 0))]
    scratch = [
        pltpu.VMEM((BAND + LANES, BAND), jnp.bfloat16),
        pltpu.VMEM((6, 8, LANES), jnp.float32),
        pltpu.VMEM((steps * count * LANES, BAND + LANES), jnp.bfloat16),
        pltpu.VMEM((steps, count, halves, LANES + 2 * SIDE, LANES), jnp.float32),
        pltpu.VMEM((steps, count * halves, LANES, LANES), jnp.float32),
        pltpu.VMEM((steps, 6, count * halves, LANES // CELL, LANES), jnp.float32),
        pltpu.VMEM((count * halves, LANES, LANES), jnp.int32),
        pltpu.VMEM((count * halves, LANES, LANES), jnp.int32),
        pltpu.VMEM((count, height, LANES), jnp.int32),
        pltpu.VMEM((count, height, LANES), jnp.int32),
    ]
    if first:
        out_shape.append(jax.ShapeDtypeStruct((LANES, height), jnp.float32))
        out_specs.append(pl.BlockSpec((LANES, BAND), lambda n: (0, n)))
        scratch.append(pltpu.VMEM((steps, width, LANES), jnp.bfloat16))
    else:
        in_specs.append(pl.BlockSpec((4 * steps, BAND), lambda n: (0, n)))
        args.append(halo)
    points = steps * height * LANES * count
    return pl.pallas_call(
        body,
        grid=(height // BAND,),
        in_specs=in_specs,
        out_specs=out_specs,
        out_shape=out_shape,
        scratch_shapes=scratch,
        compiler_params=pltpu.CompilerParams(
            dimension_semantics=("arbitrary",), vmem_limit_bytes=56 * 1024 * 1024
        ),
        cost_estimate=pl.CostEstimate(flops=40 * points, bytes_accessed=2 * points, transcendentals=3 * points),
        name="march",
    )(*args)


def blend_kernel(tiles, order_ref, got_ref, out_ref):
    ranks = got_ref.shape[0]
    count = len(tiles)
    unroll = 4
    lower = lax.broadcasted_iota(jnp.int32, (8, LANES), 0) < 4
    zero = jnp.zeros((8, LANES), jnp.float32)
    one = zero + 1.0

    def layer(i, carry):
        carry = list(carry)
        for u in range(unroll):
            d = order_ref[i * unroll + u]
            for n in range(count):
                lanes = slice(LANES * n, LANES * n + LANES)
                red, green, blue, alpha, trans, high, low, half = carry[n]
                first = got_ref[d, 0:8, lanes]
                mixed = got_ref[d, 8:16, lanes]
                last = got_ref[d, 16:24, lanes]
                cover = decode(last & 0xFFFF) * trans
                red = red + trans * decode(lax.shift_right_logical(first, 16))
                green = green + trans * decode(first & 0xFFFF)
                blue = blue + trans * decode(lax.shift_right_logical(last, 16))
                alpha = alpha + cover
                trans = trans - cover
                level = decode(mixed & 0xFFFF)
                opaque = jnp.where(lower, pltpu.roll(level, 4, 0), level)
                high = high + half * decode(lax.shift_right_logical(mixed, 16))
                low = low + half * level
                half = half - half * opaque
                carry[n] = (red, green, blue, alpha, trans, high, low, half)
        return tuple(carry)

    start = tuple((zero, zero, zero, zero, one, zero, zero, one) for _ in range(count))
    final = lax.fori_loop(0, ranks // unroll, layer, start)
    for n in range(count):
        lanes = slice(LANES * tiles[n], LANES * tiles[n] + LANES)
        red, green, blue, alpha, trans, high, low, half = final[n]
        for r in range(8):
            for c, plane in enumerate((red, green, blue, alpha)):
                out_ref[c, r, :, lanes] = plane[r : r + 1]
        for r in range(4):
            for c, plane in enumerate((high, low)):
                out_ref[c, 8 + r, :, lanes] = plane[r : r + 1]
                out_ref[2 + c, 8 + r, :, lanes] = plane[4 + r : 5 + r]


def blend(tiles, order, got, image, width):
    ranks, rows, lanes = got.shape
    whole = pl.BlockSpec(memory_space=pltpu.VMEM)
    scalars = pl.BlockSpec(memory_space=pltpu.SMEM)
    picture = jax.ShapeDtypeStruct((4, rows // 2, 1, width), jnp.float32)
    cost = pl.CostEstimate(flops=40 * got.size, bytes_accessed=4 * got.size, transcendentals=0)
    got = pltpu.with_memory_space_constraint(got, pltpu.VMEM)

    def early(place_ref, got_ref, out_ref, order_ref):
        def note(d, carry):
            order_ref[place_ref[d]] = d
            return carry

        lax.fori_loop(0, ranks, note, 0)
        blend_kernel(tiles, order_ref, got_ref, out_ref)

    def late(order_ref, got_ref, image_ref, out_ref):
        out_ref[...] = image_ref[...]
        blend_kernel(tiles, order_ref, got_ref, out_ref)

    if image is None:
        return pl.pallas_call(
            early,
            in_specs=[scalars, whole],
            out_specs=[whole, scalars],
            out_shape=[picture, jax.ShapeDtypeStruct((ranks,), jnp.int32)],
            cost_estimate=cost,
            name="blend",
        )(order, got)
    return pl.pallas_call(
        late, in_specs=[scalars, whole, whole], out_specs=whole, out_shape=picture, cost_estimate=cost, name="blend"
    )(order, got, image)


def on_device(volume, table_index, brick_position, tf_center, tf_width, tf_peak, tf_color):
    samples = volume[:, 0]
    cells = jnp.swapaxes(table_index[:, 0], 1, 2)
    steps, height, width = samples.shape
    ranks = lax.axis_size("depth")
    tables = [tf_center[None], tf_width[None], tf_peak[None], tf_color]
    tile_rank = lax.axis_index("tile")
    col_bit = tile_rank % 2
    row_bit = tile_rank // 2
    send_row = jnp.where(row_bit == 0, samples[:, height - 1, :], samples[:, 0, :])
    got_row = from_partner(send_row, "tile", 1)
    zero_row = jnp.zeros_like(got_row)
    ends = [jnp.where(row_bit == 1, got_row, zero_row)]
    for n in range(1, height // BAND):
        ends += [samples[:, BAND * n, :], samples[:, BAND * n - 1, :]]
    ends += [jnp.where(row_bit == 0, got_row, zero_row)]
    bands = height // BAND
    rim_rows = jnp.stack([jnp.stack(ends[2 * n : 2 * n + 2], axis=1) for n in range(bands)], axis=0)
    rim_rows = rim_rows.reshape(bands, 2 * steps, width)
    rim_rows = jnp.pad(rim_rows, ((0, 0), (0, LANES - 2 * steps), (0, 0)))
    early, edges = march(CHUNKS[0], ranks, tables, samples, rim_rows, cells, None)
    swap = functools.partial(lax.all_to_all, axis_name="depth", split_axis=0, concat_axis=0, tiled=True)
    got_early = swap(early)
    edges = edges[: EDGES * steps].reshape(steps, EDGES, height)
    send_col = jnp.where(col_bit == 0, edges[:, 7], edges[:, 0]).astype(jnp.bfloat16)
    got_col = from_partner(send_col, "tile", 0).astype(jnp.float32)
    zero_col = jnp.zeros_like(got_col)
    lines = [jnp.where(col_bit == 1, got_col, zero_col), edges[:, 2], edges[:, 5], jnp.where(col_bit == 0, got_col, zero_col)]
    halo = jnp.stack(lines, axis=1).reshape(4 * steps, height)
    (late,) = march(CHUNKS[1], ranks, tables, samples, rim_rows, cells, halo)
    got_late = swap(late)
    image, order = blend(CHUNKS[0], brick_position, got_early, None, width)
    image = blend(CHUNKS[1], order, got_late, image, width)
    return jnp.swapaxes(image, 1, 2)


def solution(mesh):
    return jax.shard_map(
        on_device,
        mesh=mesh,
        in_specs=(
            P("depth", "tile", None, None),
            P("depth", "tile", None, None),
            P(),
            P(),
            P(),
            P(),
            P(),
        ),
        out_specs=P(None, "tile", "depth", None),
        check_vma=False,
    )
```

```python
import functools

import jax
import jax.numpy as jnp
from jax import lax
from jax.experimental import pallas as pl
from jax.experimental.pallas import tpu as pltpu
from jax.sharding import PartitionSpec as P


CELL = 16
LANES = 128
SIDE = 8
BAND = 256
LOG2E = 1.4426950408889634
LEVELS = 65535.0
SCALE = LEVELS**4
CHUNKS = ((1, 2), (0, 3))
EDGES = 8
STRIP = 4
SHADE_GAIN = 0.7 * 0.6 * 0.6
SHADE_BASE = 0.3 / SHADE_GAIN

NN = (((1,), (0,)), ((), ()))


def from_partner(value, axis, apart):
    return lax.ppermute(value, axis, [(i, i ^ 1 << apart) for i in range(lax.axis_size(axis))])


def code(value):
    root = lax.rsqrt(lax.rsqrt(jnp.maximum(value, 0.0)))
    return jnp.minimum(root + 0.5, LEVELS).astype(jnp.int32)


def decode(word):
    root = word.astype(jnp.float32) * (1.0 / LEVELS)
    square = root * root
    return square * square


def march_kernel(tiles, spans, sizes, *refs):
    steps, height, width, total = sizes
    middle = len(spans) == 1
    count = len(tiles)
    center_ref, wide_ref, peak_ref, color_ref, vol_ref, rim_ref, index_ref, outer_ref, edge_ref = refs[:9]
    first = outer_ref is None
    out_ref, done_a, done_b = refs[9:12]
    scratch = refs[12:]
    (band_ref, table_ref, left_ref, value_ref, grad_ref, param_ref, pair_a, pair_b, turn_a, turn_b) = scratch[:10]
    part = pl.program_id(0)
    halves = BAND // LANES
    groups = LANES // CELL

    @pl.when(part == 0)
    def _():
        k = lax.broadcasted_iota(jnp.int32, (BAND + LANES, BAND), 0)
        r = lax.broadcasted_iota(jnp.int32, (BAND + LANES, BAND), 1)
        rim = k >= BAND
        above = (~rim & (k == r - 1)) | (rim & (k % 2 == 0) & (r == 0))
        below = (~rim & (k == r + 1)) | (rim & (k % 2 == 1) & (r == BAND - 1))
        band_ref[...] = jnp.where(below, 1.0, jnp.where(above, -1.0, 0.0)).astype(jnp.bfloat16)
        shape = (8, 16)
        scale = (0.5 * LOG2E) ** 0.5 / wide_ref[...]
        table_ref[0, :, 0:16] = jnp.broadcast_to(center_ref[...], shape)
        table_ref[1, :, 0:16] = jnp.broadcast_to(scale, shape)
        table_ref[2, :, 0:16] = jnp.broadcast_to(jnp.log2(peak_ref[...] * (0.25 * LOG2E / total)), shape)
        for n in range(3):
            table_ref[3 + n, :, 0:16] = jnp.broadcast_to(color_ref[n : n + 1, :] * (SHADE_GAIN * SCALE), shape)
        if first:
            spots_ref = scratch[10]
            col = lax.broadcasted_iota(jnp.int32, (width, LANES), 0)
            lane = lax.broadcasted_iota(jnp.int32, (width, LANES), 1)
            which = lane % EDGES
            want = jnp.where(which == 0, 0, (which + 1) // 2 * LANES - which % 2)
            spots_ref[...] = jnp.where(col == want, 1.0, 0.0).astype(jnp.bfloat16)

    if first:
        spots_ref = scratch[10]
        rows = vol_ref[...].reshape(steps * BAND, width)
        seen = lax.dot_general(rows, spots_ref[...], NN, preferred_element_type=jnp.float32)
        owner = lax.broadcasted_iota(jnp.int32, (BAND, LANES), 1) // EDGES
        found = jnp.zeros((BAND, LANES), jnp.float32)
        for s in range(steps):
            found = jnp.where(owner == s, seen[BAND * s : BAND * s + BAND], found)
        for m in range(halves):
            edge_ref[m] = found[LANES * m : LANES * m + LANES].T

    pair_lane = lax.broadcasted_iota(jnp.int32, (LANES, LANES), 1) // 2
    rims = [rim_ref[:, LANES * t : LANES * t + LANES].astype(jnp.float32).T for t in tiles]
    batch = 6
    for q in range(steps // batch):
        for s in range(batch * q, batch * q + batch):
            for k in range(count):
                t = tiles[k]
                at = slice((s * count + k) * LANES, (s * count + k) * LANES + LANES)
                if not first:
                    source = vol_ref[k][s]
                else:
                    source = vol_ref[s, :, LANES * t : LANES * t + LANES]
                turned = source.T
                left_ref[at, 0:BAND] = turned
                left_ref[at, BAND : BAND + LANES] = jnp.where(pair_lane == s, rims[k], 0.0).astype(jnp.bfloat16)
                for m in range(halves):
                    lanes = slice(LANES * m, LANES * m + LANES)
                    value_ref[s, k, m, SIDE : SIDE + LANES, :] = turned[:, lanes].astype(jnp.float32)
                    if t == 0:
                        before = outer_ref[0, s : s + 1, lanes]
                    else:
                        before = edge_ref[m, EDGES * s + 2 * t - 1 : EDGES * s + 2 * t, :]
                    if t == width // LANES - 1:
                        after = outer_ref[1, s : s + 1, lanes]
                    else:
                        after = edge_ref[m, EDGES * s + 2 * t + 2 : EDGES * s + 2 * t + 3, :]
                    value_ref[s, k, m, SIDE - 1 : SIDE, :] = before
                    value_ref[s, k, m, SIDE + LANES : SIDE + LANES + 1, :] = after
                    index = index_ref[s, groups * t : groups * t + groups, lanes]
                    for p in range(6):
                        param_ref[s, p, k * halves + m] = jnp.take_along_axis(table_ref[p], index, axis=1)
        size = batch * count * LANES
        grad = lax.dot_general(left_ref[q * size : q * size + size, :], band_ref[...], NN, preferred_element_type=jnp.float32)
        for s in range(batch):
            for k in range(count):
                for m in range(halves):
                    at = (s * count + k) * LANES
                    grad_ref[q * batch + s, k * halves + m] = grad[at : at + LANES, LANES * m : LANES * m + LANES]

    def strip(i, carry):
        g = i % (groups // STRIP) * STRIP
        lane = i // (groups // STRIP)
        k = lane // halves
        m = lane % halves
        base = pl.multiple_of(g * CELL, CELL)
        zero = jnp.zeros((8, LANES), jnp.float32)
        state = [[zero, zero + 1.0, zero, zero, zero] for _ in range(2 * STRIP)]
        for s in range(steps):
            for u in range(2 * STRIP):
                if u % 2 == 0:
                    param = [param_ref[s, p, lane, pl.ds(g + u // 2, 8, stride=0), :] for p in range(6)]
                depth, trans, red, green, blue = state[u]
                at = base + 8 * u
                value = value_ref[s, k, m, pl.ds(at + SIDE, 8), :]
                ahead = value_ref[s, k, m, pl.ds(at + SIDE + 1, 8), :]
                behind = value_ref[s, k, m, pl.ds(at + SIDE - 1, 8), :]
                grad_x = ahead - behind
                grad_y = grad_ref[s, lane, pl.ds(at, 8), :]
                energy = grad_x * grad_x + grad_y * grad_y
                facing = grad_x + (0.8 / 0.6) * grad_y
                shade = SHADE_BASE + facing * facing / (4.0 + energy)
                scaled = (value - param[0]) * param[1]
                rate = jnp.exp2(param[2] - scaled * scaled)
                depth = depth - rate * energy
                after = jnp.exp2(depth)
                weight = (trans - after) * shade
                red = red + weight * param[3]
                green = green + weight * param[4]
                blue = blue + weight * param[5]
                state[u] = [depth, after, red, green, blue]
        for u in range(2 * STRIP):
            depth, trans, red, green, blue = state[u]
            at = pl.ds(base + 8 * u, 8)
            pair_a[lane, at, :] = (code(red) << 16) | code(green)
            pair_b[lane, at, :] = (code(blue) << 16) | code((1.0 - trans) * SCALE)
        return carry

    lax.fori_loop(0, groups // STRIP * count * halves, strip, 0)
    for k in range(count):
        for m in range(halves):
            if middle:
                rows = slice(m * LANES, m * LANES + LANES)
                done_a[k, rows, :] = pair_a[k * halves + m].T
                done_b[k, rows, :] = pair_b[k * halves + m].T
            else:
                row = part * (BAND * (spans[1] - spans[0])) + (BAND * spans[0] + m * LANES)
                rows = pl.ds(pl.multiple_of(row, LANES), LANES)
                turn_a[k, rows, :] = pair_a[k * halves + m].T
                turn_b[k, rows, :] = pair_b[k * halves + m].T
    if middle:
        return

    @pl.when(part == len(spans) - 1)
    def _():
        if done_a is not None:
            turn_a[:, BAND : 2 * BAND, :] = done_a[...]
            turn_b[:, BAND : 2 * BAND, :] = done_b[...]
        piece = height // out_ref.shape[0]

        def pack(d, carry):
            for u in range(4):
                e = d * 4 + u
                r = e * piece
                for k in range(count):
                    lanes = slice(LANES * k, LANES * k + LANES)
                    out_ref[e, 0:8, lanes] = turn_a[k, pl.ds(r, 8), :]
                    out_ref[e, 8:12, lanes] = turn_a[k, pl.ds(r + 8, 4), :]
                    out_ref[e, 12:16, lanes] = turn_b[k, pl.ds(r + 8, 4), :]
                    out_ref[e, 16:24, lanes] = turn_b[k, pl.ds(r, 8), :]
            return carry

        lax.fori_loop(0, out_ref.shape[0] // 4, pack, 0)


def march(tiles, spans, ranks, tables, samples, rim_rows, cells, outer=None, edges=None, done=None):
    steps, height, width = samples.shape
    first = outer is None
    middle = len(spans) == 1
    count = len(tiles)
    halves = BAND // LANES
    at = lambda n: spans[0] + n * (spans[-1] - spans[0]) // max(len(spans) - 1, 1)

    def body(*refs):
        refs = list(refs)
        if not first:
            refs[4 : 4 + count] = [refs[4 : 4 + count]]
            refs[10:10] = [None, None]
        elif middle:
            done_a, done_b, edge = refs[7:10]
            refs[7:10] = [None, edge, None, done_a, done_b]
        else:
            done_a, done_b, out, edge = refs[7:11]
            refs[7:11] = [None, edge, out, done_a, done_b]
        march_kernel(tiles, spans, (steps, height, width, steps * ranks), *refs)

    small = lambda shape: pl.BlockSpec(shape, lambda n: (0,) * len(shape))
    in_specs = [small((1, 16)), small((1, 16)), small((1, 16)), small((3, 16))]
    args = list(tables)
    if first:
        in_specs.append(pl.BlockSpec((steps, BAND, width), lambda n: (0, at(n), 0)))
        args.append(samples)
    else:
        for t in tiles:
            in_specs.append(pl.BlockSpec((steps, BAND, LANES), lambda n, t=t: (0, at(n), t)))
            args.append(samples)
    in_specs += [
        pl.BlockSpec((None, LANES, width), lambda n: (n, 0, 0)),
        pl.BlockSpec((steps, width // CELL, BAND), lambda n: (0, 0, at(n))),
    ]
    args += [rim_rows, cells]
    shape = (ranks, 2 * height // ranks, LANES * count)
    half = (count, BAND, LANES)
    if middle:
        out_shape = [jax.ShapeDtypeStruct(half, jnp.int32)] * 2
        out_specs = [small(half)] * 2
    else:
        out_shape = [jax.ShapeDtypeStruct(shape, jnp.int32)]
        out_specs = [small(shape)]
    scratch = [
        pltpu.VMEM((BAND + LANES, BAND), jnp.bfloat16),
        pltpu.VMEM((6, 8, LANES), jnp.float32),
        pltpu.VMEM((steps * count * LANES, BAND + LANES), jnp.bfloat16),
        pltpu.VMEM((steps, count, halves, LANES + 2 * SIDE, LANES), jnp.float32),
        pltpu.VMEM((steps, count * halves, LANES, LANES), jnp.float32),
        pltpu.VMEM((steps, 6, count * halves, LANES // CELL, LANES), jnp.float32),
        pltpu.VMEM((count * halves, LANES, LANES), jnp.int32),
        pltpu.VMEM((count * halves, LANES, LANES), jnp.int32),
        pltpu.VMEM((count, height, LANES), jnp.int32),
        pltpu.VMEM((count, height, LANES), jnp.int32),
    ]
    if first:
        out_shape.append(jax.ShapeDtypeStruct((len(spans) * halves, LANES, LANES), jnp.float32))
        out_specs.append(pl.BlockSpec((halves, LANES, LANES), lambda n: (n, 0, 0)))
        scratch.append(pltpu.VMEM((width, LANES), jnp.bfloat16))
        if done is not None:
            in_specs += [small(half)] * 2
            args += done
    else:
        in_specs.append(pl.BlockSpec((2, 16, BAND), lambda n: (0, 0, n)))
        in_specs.append(pl.BlockSpec((halves, LANES, LANES), lambda n: (n, 0, 0)))
        args += [outer, edges]
    points = steps * BAND * len(spans) * LANES * count
    return pl.pallas_call(
        body,
        grid=(len(spans),),
        in_specs=in_specs,
        out_specs=out_specs,
        out_shape=out_shape,
        scratch_shapes=scratch,
        compiler_params=pltpu.CompilerParams(
            dimension_semantics=("arbitrary",), vmem_limit_bytes=56 * 1024 * 1024
        ),
        cost_estimate=pl.CostEstimate(flops=40 * points, bytes_accessed=2 * points, transcendentals=3 * points),
        name="march",
    )(*args)


def blend_kernel(tiles, order_ref, got_ref, out_ref):
    ranks = got_ref.shape[0]
    count = len(tiles)
    unroll = 4
    lower = lax.broadcasted_iota(jnp.int32, (8, LANES), 0) < 4
    zero = jnp.zeros((8, LANES), jnp.float32)
    one = zero + 1.0

    def layer(i, carry):
        carry = list(carry)
        for u in range(unroll):
            d = order_ref[i * unroll + u]
            for n in range(count):
                lanes = slice(LANES * n, LANES * n + LANES)
                red, green, blue, alpha, trans, high, low, half = carry[n]
                first = got_ref[d, 0:8, lanes]
                mixed = got_ref[d, 8:16, lanes]
                last = got_ref[d, 16:24, lanes]
                cover = decode(last & 0xFFFF) * trans
                red = red + trans * decode(lax.shift_right_logical(first, 16))
                green = green + trans * decode(first & 0xFFFF)
                blue = blue + trans * decode(lax.shift_right_logical(last, 16))
                alpha = alpha + cover
                trans = trans - cover
                level = decode(mixed & 0xFFFF)
                opaque = jnp.where(lower, pltpu.roll(level, 4, 0), level)
                high = high + half * decode(lax.shift_right_logical(mixed, 16))
                low = low + half * level
                half = half - half * opaque
                carry[n] = (red, green, blue, alpha, trans, high, low, half)
        return tuple(carry)

    start = tuple((zero, zero, zero, zero, one, zero, zero, one) for _ in range(count))
    final = lax.fori_loop(0, ranks // unroll, layer, start)
    for n in range(count):
        lanes = slice(LANES * tiles[n], LANES * tiles[n] + LANES)
        red, green, blue, alpha, _, high, low, _ = final[n]
        for r in range(8):
            for c, plane in enumerate((red, green, blue, alpha)):
                out_ref[c, r, :, lanes] = plane[r : r + 1]
        for r in range(4):
            for c, plane in enumerate((high, low)):
                out_ref[c, 8 + r, :, lanes] = plane[r : r + 1]
                out_ref[2 + c, 8 + r, :, lanes] = plane[4 + r : 5 + r]


def blend(tiles, order, got, image, width):
    ranks, rows, _ = got.shape
    whole = pl.BlockSpec(memory_space=pltpu.VMEM)
    scalars = pl.BlockSpec(memory_space=pltpu.SMEM)
    picture = jax.ShapeDtypeStruct((4, rows // 2, 1, width), jnp.float32)
    cost = pl.CostEstimate(flops=40 * got.size, bytes_accessed=4 * got.size, transcendentals=0)
    got = pltpu.with_memory_space_constraint(got, pltpu.VMEM)

    def early(place_ref, got_ref, out_ref, order_ref):
        def note(d, carry):
            order_ref[place_ref[d]] = d
            return carry

        lax.fori_loop(0, ranks, note, 0)
        blend_kernel(tiles, order_ref, got_ref, out_ref)

    def late(order_ref, got_ref, image_ref, out_ref):
        out_ref[...] = image_ref[...]
        blend_kernel(tiles, order_ref, got_ref, out_ref)

    if image is None:
        return pl.pallas_call(
            early,
            in_specs=[scalars, whole],
            out_specs=[whole, scalars],
            out_shape=[picture, jax.ShapeDtypeStruct((ranks,), jnp.int32)],
            cost_estimate=cost,
            name="blend",
        )(order, got)
    return pl.pallas_call(
        late, in_specs=[scalars, whole, whole], out_specs=whole, out_shape=picture, cost_estimate=cost, name="blend"
    )(order, got, image)


def on_device(volume, table_index, brick_position, tf_center, tf_width, tf_peak, tf_color):
    samples = volume[:, 0]
    cells = jnp.swapaxes(table_index[:, 0], 1, 2)
    steps, height, width = samples.shape
    ranks = lax.axis_size("depth")
    tables = [tf_center[None], tf_width[None], tf_peak[None], tf_color]
    tile_rank = lax.axis_index("tile")
    col_bit = tile_rank % 2
    row_bit = tile_rank // 2
    bands = height // BAND
    bare = [samples[:, n, :] for n in range(height) if 0 < n and n % BAND in (0, BAND - 1) and n < height - 1]
    pad = ((0, 0), (0, LANES - 2 * steps), (0, 0))
    send_row = jnp.where(row_bit == 0, samples[:, height - 1, :], samples[:, 0, :])
    inner_rows = jnp.pad(jnp.stack(bare[0:1] + bare[3:4], axis=1).reshape(1, 2 * steps, width), pad)
    got_row = from_partner(send_row, "tile", 1)
    *done, middle = march(CHUNKS[0], (1,), ranks, tables, samples, inner_rows, cells)
    zero_row = jnp.zeros_like(got_row)
    above = [jnp.where(row_bit == 1, got_row, zero_row), bare[1]]
    below = [bare[2], jnp.where(row_bit == 0, got_row, zero_row)]
    outer_rows = jnp.stack([jnp.stack(above, axis=1), jnp.stack(below, axis=1)], axis=0)
    outer_rows = jnp.pad(outer_rows.reshape(2, 2 * steps, width), pad)
    early, ends = march(CHUNKS[0], (0, bands - 1), ranks, tables, samples, outer_rows, cells, done=done)
    swap = functools.partial(lax.all_to_all, axis_name="depth", split_axis=0, concat_axis=0, tiled=True)
    got_early = swap(early)
    halves = BAND // LANES
    edges = jnp.concatenate([ends[:halves], middle, ends[halves:]], axis=0)
    marks = edges[:, : EDGES * steps].reshape(height // LANES, steps, EDGES, LANES)
    marks = jnp.where(col_bit == 0, marks[:, :, EDGES - 1], marks[:, :, 0])
    send_col = jnp.swapaxes(marks, 0, 1).reshape(steps, height).astype(jnp.bfloat16)
    got_col = jnp.pad(from_partner(send_col, "tile", 0).astype(jnp.float32), ((0, 16 - steps), (0, 0)))
    outer = jnp.stack([jnp.where(col_bit == 1, got_col, 0.0), jnp.where(col_bit == 0, got_col, 0.0)], axis=0)
    rows = jnp.concatenate([outer_rows[:1], inner_rows, outer_rows[1:]], axis=0)
    (late,) = march(CHUNKS[1], tuple(range(bands)), ranks, tables, samples, rows, cells, outer, edges)
    got_late = swap(late)
    image, order = blend(CHUNKS[0], brick_position, got_early, None, width)
    image = blend(CHUNKS[1], order, got_late, image, width)
    return jnp.swapaxes(image, 1, 2)


def solution(mesh):
    return jax.shard_map(
        on_device,
        mesh=mesh,
        in_specs=(
            P("depth", "tile", None, None),
            P("depth", "tile", None, None),
            P(),
            P(),
            P(),
            P(),
            P(),
        ),
        out_specs=P(None, "tile", "depth", None),
        check_vma=False,
    )
```

```python
import functools

import jax
import jax.numpy as jnp
from jax import lax
from jax.experimental import pallas as pl
from jax.experimental.pallas import tpu as pltpu
from jax.sharding import PartitionSpec as P


CELL = 16
LANES = 128
SIDE = 8
BAND = 256
LOG2E = 1.4426950408889634
LEVELS = 65535.0
SCALE = LEVELS**4
CHUNKS = ((1,), (0, 2, 3))
EDGES = 8
STRIP = 4
LIGHT = 32
RIMS = LANES
SHADE_GAIN = 0.7 * 0.6 * 0.6
SHADE_BASE = 0.3 / SHADE_GAIN

NN = (((1,), (0,)), ((), ()))


def from_partner(value, axis, apart):
    return lax.ppermute(value, axis, [(i, i ^ 1 << apart) for i in range(lax.axis_size(axis))])


def code(value):
    root = lax.rsqrt(lax.rsqrt(jnp.maximum(value, 0.0)))
    return (root + 0.5).astype(jnp.int32)


def decode(word):
    root = word.astype(jnp.float32) * (1.0 / LEVELS)
    square = root * root
    return square * square


def march_kernel(tiles, spans, sizes, *refs):
    steps, height, width, total = sizes
    middle = len(spans) == 1
    count = len(tiles)
    center_ref, wide_ref, peak_ref, color_ref, vol_ref, rim_ref, index_ref, outer_ref, edge_ref = refs[:9]
    first = outer_ref is None
    out_ref, done_a, done_b = refs[9:12]
    scratch = refs[12:]
    (band_ref, ends_ref, table_ref, left_ref, value_ref, energy_ref, shade_ref, param_ref, pair_a, pair_b, turn_a, turn_b) = scratch[:12]
    part = pl.program_id(0)
    halves = BAND // LANES
    groups = LANES // CELL

    @pl.when(part == 0)
    def _():
        k = lax.broadcasted_iota(jnp.int32, (BAND, BAND), 0)
        r = lax.broadcasted_iota(jnp.int32, (BAND, BAND), 1)
        band_ref[...] = jnp.where(k == r + 1, 1.0, jnp.where(k == r - 1, -1.0, 0.0)).astype(jnp.bfloat16)
        k = lax.broadcasted_iota(jnp.int32, (RIMS, BAND), 0)
        r = lax.broadcasted_iota(jnp.int32, (RIMS, BAND), 1)
        edge = jnp.where(r == 0, -1.0, 0.0), jnp.where(r == BAND - 1, 1.0, 0.0)
        for s in range(steps):
            ends = jnp.where(k == 2 * s, edge[0], jnp.where(k == 2 * s + 1, edge[1], 0.0))
            ends_ref[s] = ends.astype(jnp.bfloat16)
        shape = (8, 16)
        scale = (0.5 * LOG2E) ** 0.5 / wide_ref[...]
        table_ref[0, :, 0:16] = jnp.broadcast_to(center_ref[...], shape)
        table_ref[1, :, 0:16] = jnp.broadcast_to(scale, shape)
        table_ref[2, :, 0:16] = jnp.broadcast_to(jnp.log2(peak_ref[...] * (0.25 * LOG2E / total)), shape)
        for n in range(3):
            table_ref[3 + n, :, 0:16] = jnp.broadcast_to(color_ref[n : n + 1, :] * (SHADE_GAIN * SCALE), shape)
        if first:
            spots_ref = scratch[12]
            col = lax.broadcasted_iota(jnp.int32, (width, LANES), 0)
            lane = lax.broadcasted_iota(jnp.int32, (width, LANES), 1)
            which = lane % EDGES
            want = jnp.where(which == 0, 0, (which + 1) // 2 * LANES - which % 2)
            spots_ref[...] = jnp.where(col == want, 1.0, 0.0).astype(jnp.bfloat16)

    if first:
        spots_ref = scratch[12]
        rows = vol_ref[...].reshape(steps * BAND, width)
        seen = lax.dot_general(rows, spots_ref[...], NN, preferred_element_type=jnp.float32)
        owner = lax.broadcasted_iota(jnp.int32, (BAND, LANES), 1) // EDGES
        found = jnp.zeros((BAND, LANES), jnp.float32)
        for s in range(steps):
            found = jnp.where(owner == s, seen[BAND * s : BAND * s + BAND], found)
        for m in range(halves):
            edge_ref[m] = found[LANES * m : LANES * m + LANES].T

    for k, t in enumerate(tiles):
        rims = rim_ref[:, LANES * t : LANES * t + LANES].T
        for n in range(2):
            left_ref[n, LANES * k : LANES * k + LANES, BAND : BAND + RIMS] = rims[:, 0:RIMS]

    def turn(s):
        for k in range(count):
            t = tiles[k]
            at = slice(k * LANES, k * LANES + LANES)
            source = vol_ref[s, :, LANES * t : LANES * t + LANES] if first else vol_ref[k][s]
            turned = source.T
            left_ref[s % 2, at, 0:BAND] = turned
            for m in range(halves):
                lanes = slice(LANES * m, LANES * m + LANES)
                value_ref[s, k, m, SIDE : SIDE + LANES, :] = turned[:, lanes].astype(jnp.float32)
                if t == 0:
                    before = outer_ref[0, s : s + 1, lanes]
                else:
                    before = edge_ref[m, EDGES * s + 2 * t - 1 : EDGES * s + 2 * t, :]
                if t == width // LANES - 1:
                    after = outer_ref[1, s : s + 1, lanes]
                else:
                    after = edge_ref[m, EDGES * s + 2 * t + 2 : EDGES * s + 2 * t + 3, :]
                value_ref[s, k, m, SIDE - 1 : SIDE, :] = before
                value_ref[s, k, m, SIDE + LANES : SIDE + LANES + 1, :] = after
                index = index_ref[s, groups * t : groups * t + groups, lanes]
                for p in range(6):
                    param_ref[s, p, k * halves + m] = jnp.take_along_axis(table_ref[p], index, axis=1)
        right = jnp.concatenate([band_ref[...], ends_ref[s]], axis=0)
        return lax.dot_general(left_ref[s % 2], right, NN, preferred_element_type=jnp.float32)

    def light(s, grad):
        for k in range(count):
            for m in range(halves):
                lane = k * halves + m
                for c in range(0, LANES, LIGHT):
                    ahead = value_ref[s, k, m, SIDE + 1 + c : SIDE + 1 + c + LIGHT, :]
                    behind = value_ref[s, k, m, SIDE - 1 + c : SIDE - 1 + c + LIGHT, :]
                    grad_x = ahead - behind
                    grad_y = grad[k * LANES + c : k * LANES + c + LIGHT, LANES * m : LANES * m + LANES]
                    energy = grad_x * grad_x + grad_y * grad_y
                    facing = grad_x + (0.8 / 0.6) * grad_y
                    energy_ref[s, lane, c : c + LIGHT, :] = energy
                    shade_ref[s, lane, c : c + LIGHT, :] = SHADE_BASE + facing * facing / (4.0 + energy)

    grad = turn(0)
    for s in range(steps):
        ready = grad
        if s + 1 < steps:
            grad = turn(s + 1)
        light(s, ready)

    def strip(i, carry):
        g = i % (groups // STRIP) * STRIP
        lane = i // (groups // STRIP)
        k = lane // halves
        m = lane % halves
        base = pl.multiple_of(g * CELL, CELL)
        zero = jnp.zeros((8, LANES), jnp.float32)
        state = [[zero, zero + 1.0, zero, zero, zero] for _ in range(2 * STRIP)]
        for s in range(steps):
            for u in range(2 * STRIP):
                if u % 2 == 0:
                    param = [param_ref[s, p, lane, pl.ds(g + u // 2, 8, stride=0), :] for p in range(6)]
                depth, trans, red, green, blue = state[u]
                at = base + 8 * u
                value = value_ref[s, k, m, pl.ds(at + SIDE, 8), :]
                energy = energy_ref[s, lane, pl.ds(at, 8), :]
                shade = shade_ref[s, lane, pl.ds(at, 8), :]
                scaled = (value - param[0]) * param[1]
                rate = jnp.exp2(param[2] - scaled * scaled)
                depth = depth - rate * energy
                after = jnp.exp2(depth)
                weight = (trans - after) * shade
                red = red + weight * param[3]
                green = green + weight * param[4]
                blue = blue + weight * param[5]
                state[u] = [depth, after, red, green, blue]
        for u in range(2 * STRIP):
            depth, trans, red, green, blue = state[u]
            at = pl.ds(base + 8 * u, 8)
            pair_a[lane, at, :] = (code(red) << 16) | code(green)
            pair_b[lane, at, :] = (code(blue) << 16) | code((1.0 - trans) * SCALE)
        return carry

    lax.fori_loop(0, groups // STRIP * count * halves, strip, 0)
    for k in range(count):
        for m in range(halves):
            if middle:
                rows = slice(m * LANES, m * LANES + LANES)
                done_a[k, rows, :] = pair_a[k * halves + m].T
                done_b[k, rows, :] = pair_b[k * halves + m].T
            else:
                row = part * (BAND * (spans[1] - spans[0])) + (BAND * spans[0] + m * LANES)
                rows = pl.ds(pl.multiple_of(row, LANES), LANES)
                turn_a[k, rows, :] = pair_a[k * halves + m].T
                turn_b[k, rows, :] = pair_b[k * halves + m].T
    if middle:
        return

    @pl.when(part == len(spans) - 1)
    def _():
        if done_a is not None:
            turn_a[:, BAND : 2 * BAND, :] = done_a[...]
            turn_b[:, BAND : 2 * BAND, :] = done_b[...]
        piece = height // out_ref.shape[0]

        def pack(d, carry):
            for u in range(4):
                e = d * 4 + u
                r = e * piece
                for k in range(count):
                    lanes = slice(LANES * k, LANES * k + LANES)
                    out_ref[e, 0:8, lanes] = turn_a[k, pl.ds(r, 8), :]
                    out_ref[e, 8:12, lanes] = turn_a[k, pl.ds(r + 8, 4), :]
                    out_ref[e, 12:16, lanes] = turn_b[k, pl.ds(r + 8, 4), :]
                    out_ref[e, 16:24, lanes] = turn_b[k, pl.ds(r, 8), :]
            return carry

        lax.fori_loop(0, out_ref.shape[0] // 4, pack, 0)


def march(tiles, spans, ranks, tables, samples, rim_rows, cells, outer=None, edges=None, done=None):
    steps, height, width = samples.shape
    first = outer is None
    middle = len(spans) == 1
    count = len(tiles)
    halves = BAND // LANES
    at = lambda n: spans[0] + n * (spans[-1] - spans[0]) // max(len(spans) - 1, 1)

    def body(*refs):
        refs = list(refs)
        if not first:
            refs[4 : 4 + count] = [refs[4 : 4 + count]]
            refs[10:10] = [None, None]
        elif middle:
            done_a, done_b, edge = refs[7:10]
            refs[7:10] = [None, edge, None, done_a, done_b]
        else:
            done_a, done_b, out, edge = refs[7:11]
            refs[7:11] = [None, edge, out, done_a, done_b]
        march_kernel(tiles, spans, (steps, height, width, steps * ranks), *refs)

    small = lambda shape: pl.BlockSpec(shape, lambda n: (0,) * len(shape))
    in_specs = [small((1, 16)), small((1, 16)), small((1, 16)), small((3, 16))]
    args = list(tables)
    if first:
        in_specs.append(pl.BlockSpec((steps, BAND, width), lambda n: (0, at(n), 0)))
        args.append(samples)
    else:
        for t in tiles:
            in_specs.append(pl.BlockSpec((steps, BAND, LANES), lambda n, t=t: (0, at(n), t)))
            args.append(samples)
    in_specs += [
        pl.BlockSpec((None, LANES, width), lambda n: (n, 0, 0)),
        pl.BlockSpec((steps, width // CELL, BAND), lambda n: (0, 0, at(n))),
    ]
    args += [rim_rows, cells]
    shape = (ranks, 2 * height // ranks, LANES * count)
    half = (count, BAND, LANES)
    if middle:
        out_shape = [jax.ShapeDtypeStruct(half, jnp.int32)] * 2
        out_specs = [small(half)] * 2
    else:
        out_shape = [jax.ShapeDtypeStruct(shape, jnp.int32)]
        out_specs = [small(shape)]
    scratch = [
        pltpu.VMEM((BAND, BAND), jnp.bfloat16),
        pltpu.VMEM((steps, RIMS, BAND), jnp.bfloat16),
        pltpu.VMEM((6, 8, LANES), jnp.float32),
        pltpu.VMEM((2, count * LANES, BAND + RIMS), jnp.bfloat16),
        pltpu.VMEM((steps, count, halves, LANES + 2 * SIDE, LANES), jnp.float32),
        pltpu.VMEM((steps, count * halves, LANES, LANES), jnp.float32),
        pltpu.VMEM((steps, count * halves, LANES, LANES), jnp.float32),
        pltpu.VMEM((steps, 6, count * halves, LANES // CELL, LANES), jnp.float32),
        pltpu.VMEM((count * halves, LANES, LANES), jnp.int32),
        pltpu.VMEM((count * halves, LANES, LANES), jnp.int32),
        pltpu.VMEM((count, height, LANES), jnp.int32),
        pltpu.VMEM((count, height, LANES), jnp.int32),
    ]
    if first:
        out_shape.append(jax.ShapeDtypeStruct((len(spans) * halves, LANES, LANES), jnp.float32))
        out_specs.append(pl.BlockSpec((halves, LANES, LANES), lambda n: (n, 0, 0)))
        scratch.append(pltpu.VMEM((width, LANES), jnp.bfloat16))
        if done is not None:
            in_specs += [small(half)] * 2
            args += done
    else:
        in_specs.append(pl.BlockSpec((2, 16, BAND), lambda n: (0, 0, n)))
        in_specs.append(pl.BlockSpec((halves, LANES, LANES), lambda n: (n, 0, 0)))
        args += [outer, edges]
    points = steps * BAND * len(spans) * LANES * count
    return pl.pallas_call(
        body,
        grid=(len(spans),),
        in_specs=in_specs,
        out_specs=out_specs,
        out_shape=out_shape,
        scratch_shapes=scratch,
        compiler_params=pltpu.CompilerParams(
            dimension_semantics=("arbitrary",), vmem_limit_bytes=56 * 1024 * 1024
        ),
        cost_estimate=pl.CostEstimate(flops=40 * points, bytes_accessed=2 * points, transcendentals=3 * points),
        name="march",
    )(*args)


def blend_kernel(tiles, order_ref, got_ref, out_ref):
    ranks = got_ref.shape[0]
    count = len(tiles)
    unroll = 4
    lower = lax.broadcasted_iota(jnp.int32, (8, LANES), 0) < 4
    zero = jnp.zeros((8, LANES), jnp.float32)
    one = zero + 1.0

    def layer(i, carry):
        carry = list(carry)
        for u in range(unroll):
            d = order_ref[i * unroll + u]
            for n in range(count):
                lanes = slice(LANES * n, LANES * n + LANES)
                red, green, blue, alpha, trans, high, low, half = carry[n]
                first = got_ref[d, 0:8, lanes]
                mixed = got_ref[d, 8:16, lanes]
                last = got_ref[d, 16:24, lanes]
                cover = decode(last & 0xFFFF) * trans
                red = red + trans * decode(lax.shift_right_logical(first, 16))
                green = green + trans * decode(first & 0xFFFF)
                blue = blue + trans * decode(lax.shift_right_logical(last, 16))
                alpha = alpha + cover
                trans = trans - cover
                level = decode(mixed & 0xFFFF)
                opaque = jnp.where(lower, pltpu.roll(level, 4, 0), level)
                high = high + half * decode(lax.shift_right_logical(mixed, 16))
                low = low + half * level
                half = half - half * opaque
                carry[n] = (red, green, blue, alpha, trans, high, low, half)
        return tuple(carry)

    start = tuple((zero, zero, zero, zero, one, zero, zero, one) for _ in range(count))
    final = lax.fori_loop(0, ranks // unroll, layer, start)
    for n in range(count):
        lanes = slice(LANES * tiles[n], LANES * tiles[n] + LANES)
        red, green, blue, alpha, _, high, low, _ = final[n]
        for r in range(8):
            for c, plane in enumerate((red, green, blue, alpha)):
                out_ref[c, r, :, lanes] = plane[r : r + 1]
        for r in range(4):
            for c, plane in enumerate((high, low)):
                out_ref[c, 8 + r, :, lanes] = plane[r : r + 1]
                out_ref[2 + c, 8 + r, :, lanes] = plane[4 + r : 5 + r]


def blend(tiles, order, got, image, width):
    ranks, rows, _ = got.shape
    whole = pl.BlockSpec(memory_space=pltpu.VMEM)
    scalars = pl.BlockSpec(memory_space=pltpu.SMEM)
    picture = jax.ShapeDtypeStruct((4, rows // 2, 1, width), jnp.float32)
    cost = pl.CostEstimate(flops=40 * got.size, bytes_accessed=4 * got.size, transcendentals=0)
    got = pltpu.with_memory_space_constraint(got, pltpu.VMEM)

    def early(place_ref, got_ref, out_ref, order_ref):
        def note(d, carry):
            order_ref[place_ref[d]] = d
            return carry

        lax.fori_loop(0, ranks, note, 0)
        blend_kernel(tiles, order_ref, got_ref, out_ref)

    def late(order_ref, got_ref, image_ref, out_ref):
        out_ref[...] = image_ref[...]
        blend_kernel(tiles, order_ref, got_ref, out_ref)

    if image is None:
        return pl.pallas_call(
            early,
            in_specs=[scalars, whole],
            out_specs=[whole, scalars],
            out_shape=[picture, jax.ShapeDtypeStruct((ranks,), jnp.int32)],
            cost_estimate=cost,
            name="blend",
        )(order, got)
    return pl.pallas_call(
        late, in_specs=[scalars, whole, whole], out_specs=whole, out_shape=picture, cost_estimate=cost, name="blend"
    )(order, got, image)


def on_device(volume, table_index, brick_position, tf_center, tf_width, tf_peak, tf_color):
    samples = volume[:, 0]
    cells = jnp.swapaxes(table_index[:, 0], 1, 2)
    steps, height, width = samples.shape
    ranks = lax.axis_size("depth")
    tables = [tf_center[None], tf_width[None], tf_peak[None], tf_color]
    tile_rank = lax.axis_index("tile")
    col_bit = tile_rank % 2
    row_bit = tile_rank // 2
    bands = height // BAND
    bare = [samples[:, n, :] for n in range(height) if 0 < n and n % BAND in (0, BAND - 1) and n < height - 1]
    pad = ((0, 0), (0, LANES - 2 * steps), (0, 0))
    send_row = jnp.where(row_bit == 0, samples[:, height - 1, :], samples[:, 0, :])
    inner_rows = jnp.pad(jnp.stack(bare[0:1] + bare[3:4], axis=1).reshape(1, 2 * steps, width), pad)
    got_row = from_partner(send_row, "tile", 1)
    *done, middle = march(CHUNKS[0], (1,), ranks, tables, samples, inner_rows, cells)
    zero_row = jnp.zeros_like(got_row)
    above = [jnp.where(row_bit == 1, got_row, zero_row), bare[1]]
    below = [bare[2], jnp.where(row_bit == 0, got_row, zero_row)]
    outer_rows = jnp.stack([jnp.stack(above, axis=1), jnp.stack(below, axis=1)], axis=0)
    outer_rows = jnp.pad(outer_rows.reshape(2, 2 * steps, width), pad)
    early, ends = march(CHUNKS[0], (0, bands - 1), ranks, tables, samples, outer_rows, cells, done=done)
    swap = functools.partial(lax.all_to_all, axis_name="depth", split_axis=0, concat_axis=0, tiled=True)
    got_early = swap(early)
    halves = BAND // LANES
    edges = jnp.concatenate([ends[:halves], middle, ends[halves:]], axis=0)
    marks = edges[:, : EDGES * steps].reshape(height // LANES, steps, EDGES, LANES)
    marks = jnp.where(col_bit == 0, marks[:, :, EDGES - 1], marks[:, :, 0])
    send_col = jnp.swapaxes(marks, 0, 1).reshape(steps, height).astype(jnp.bfloat16)
    got_col = jnp.pad(from_partner(send_col, "tile", 0).astype(jnp.float32), ((0, 16 - steps), (0, 0)))
    outer = jnp.stack([jnp.where(col_bit == 1, got_col, 0.0), jnp.where(col_bit == 0, got_col, 0.0)], axis=0)
    rows = jnp.concatenate([outer_rows[:1], inner_rows, outer_rows[1:]], axis=0)
    (late,) = march(CHUNKS[1], tuple(range(bands)), ranks, tables, samples, rows, cells, outer, edges)
    got_late = swap(late)
    image, order = blend(CHUNKS[0], brick_position, got_early, None, width)
    image = blend(CHUNKS[1], order, got_late, image, width)
    return jnp.swapaxes(image, 1, 2)


def solution(mesh):
    return jax.shard_map(
        on_device,
        mesh=mesh,
        in_specs=(
            P("depth", "tile", None, None),
            P("depth", "tile", None, None),
            P(),
            P(),
            P(),
            P(),
            P(),
        ),
        out_specs=P(None, "tile", "depth", None),
        check_vma=False,
    )
```

```python
import functools

import jax
import jax.numpy as jnp
from jax import lax
from jax.experimental import pallas as pl
from jax.experimental.pallas import tpu as pltpu
from jax.sharding import PartitionSpec as P


CELL = 16
LANES = 128
SIDE = 8
BAND = 256
LOG2E = 1.4426950408889634
LEVELS = 65535.0
SCALE = LEVELS**4
CHUNKS = ((1, 2), (0, 3))
EDGES = 8
STRIP = 4
LIGHT = 32
RIMS = LANES
SHADE_GAIN = 0.7 * 0.6 * 0.6
SHADE_BASE = 0.3 / SHADE_GAIN

NN = (((1,), (0,)), ((), ()))


def from_partner(value, axis, apart):
    return lax.ppermute(value, axis, [(i, i ^ 1 << apart) for i in range(lax.axis_size(axis))])


def code(value):
    root = lax.rsqrt(lax.rsqrt(jnp.maximum(value, 0.0)))
    return (root + 0.5).astype(jnp.int32)


def decode(word):
    root = word.astype(jnp.float32) * (1.0 / LEVELS)
    square = root * root
    return square * square


def march_kernel(tiles, spans, sizes, *refs):
    steps, height, width, total = sizes
    middle = len(spans) == 1
    count = len(tiles)
    center_ref, wide_ref, peak_ref, color_ref, vol_ref, rim_ref, index_ref, outer_ref, edge_ref = refs[:9]
    first = outer_ref is None
    out_ref, done_a, done_b = refs[9:12]
    scratch = refs[12:]
    (band_ref, ends_ref, table_ref, left_ref, value_ref, energy_ref, shade_ref, param_ref, pair_a, pair_b, turn_a, turn_b) = scratch[:12]
    part = pl.program_id(0)
    halves = BAND // LANES
    groups = LANES // CELL

    @pl.when(part == 0)
    def _():
        k = lax.broadcasted_iota(jnp.int32, (BAND, BAND), 0)
        r = lax.broadcasted_iota(jnp.int32, (BAND, BAND), 1)
        band_ref[...] = jnp.where(k == r + 1, 1.0, jnp.where(k == r - 1, -1.0, 0.0)).astype(jnp.bfloat16)
        k = lax.broadcasted_iota(jnp.int32, (RIMS, BAND), 0)
        r = lax.broadcasted_iota(jnp.int32, (RIMS, BAND), 1)
        edge = jnp.where(r == 0, -1.0, 0.0), jnp.where(r == BAND - 1, 1.0, 0.0)
        for s in range(steps):
            ends = jnp.where(k == 2 * s, edge[0], jnp.where(k == 2 * s + 1, edge[1], 0.0))
            ends_ref[s] = ends.astype(jnp.bfloat16)
        shape = (8, 16)
        scale = (0.5 * LOG2E) ** 0.5 / wide_ref[...]
        table_ref[0, :, 0:16] = jnp.broadcast_to(center_ref[...], shape)
        table_ref[1, :, 0:16] = jnp.broadcast_to(scale, shape)
        table_ref[2, :, 0:16] = jnp.broadcast_to(jnp.log2(peak_ref[...] * (0.25 * LOG2E / total)), shape)
        for n in range(3):
            table_ref[3 + n, :, 0:16] = jnp.broadcast_to(color_ref[n : n + 1, :] * (SHADE_GAIN * SCALE), shape)
        if first:
            spots_ref = scratch[12]
            col = lax.broadcasted_iota(jnp.int32, (width, LANES), 0)
            lane = lax.broadcasted_iota(jnp.int32, (width, LANES), 1)
            which = lane % EDGES
            want = jnp.where(which == 0, 0, (which + 1) // 2 * LANES - which % 2)
            spots_ref[...] = jnp.where(col == want, 1.0, 0.0).astype(jnp.bfloat16)

    if first:
        spots_ref = scratch[12]
        rows = vol_ref[...].reshape(steps * BAND, width)
        seen = lax.dot_general(rows, spots_ref[...], NN, preferred_element_type=jnp.float32)
        owner = lax.broadcasted_iota(jnp.int32, (BAND, LANES), 1) // EDGES
        found = jnp.zeros((BAND, LANES), jnp.float32)
        for s in range(steps):
            found = jnp.where(owner == s, seen[BAND * s : BAND * s + BAND], found)
        for m in range(halves):
            edge_ref[m] = found[LANES * m : LANES * m + LANES].T

    for k, t in enumerate(tiles):
        rims = rim_ref[:, LANES * t : LANES * t + LANES].T
        for n in range(2):
            left_ref[n, LANES * k : LANES * k + LANES, BAND : BAND + RIMS] = rims[:, 0:RIMS]

    def turn(s):
        for k in range(count):
            t = tiles[k]
            at = slice(k * LANES, k * LANES + LANES)
            source = vol_ref[s, :, LANES * t : LANES * t + LANES] if first else vol_ref[k][s]
            turned = source.T
            left_ref[s % 2, at, 0:BAND] = turned
            for m in range(halves):
                lanes = slice(LANES * m, LANES * m + LANES)
                value_ref[s, k, m, SIDE : SIDE + LANES, :] = turned[:, lanes].astype(jnp.float32)
                if t == 0:
                    before = outer_ref[0, s : s + 1, lanes]
                else:
                    before = edge_ref[m, EDGES * s + 2 * t - 1 : EDGES * s + 2 * t, :]
                if t == width // LANES - 1:
                    after = outer_ref[1, s : s + 1, lanes]
                else:
                    after = edge_ref[m, EDGES * s + 2 * t + 2 : EDGES * s + 2 * t + 3, :]
                value_ref[s, k, m, SIDE - 1 : SIDE, :] = before
                value_ref[s, k, m, SIDE + LANES : SIDE + LANES + 1, :] = after
                index = index_ref[s, groups * t : groups * t + groups, lanes]
                for p in range(6):
                    param_ref[s, p, k * halves + m] = jnp.take_along_axis(table_ref[p], index, axis=1)
        right = jnp.concatenate([band_ref[...], ends_ref[s]], axis=0)
        return lax.dot_general(left_ref[s % 2], right, NN, preferred_element_type=jnp.float32)

    def light(s, grad):
        for k in range(count):
            for m in range(halves):
                lane = k * halves + m
                for c in range(0, LANES, LIGHT):
                    ahead = value_ref[s, k, m, SIDE + 1 + c : SIDE + 1 + c + LIGHT, :]
                    behind = value_ref[s, k, m, SIDE - 1 + c : SIDE - 1 + c + LIGHT, :]
                    grad_x = ahead - behind
                    grad_y = grad[k * LANES + c : k * LANES + c + LIGHT, LANES * m : LANES * m + LANES]
                    energy = grad_x * grad_x + grad_y * grad_y
                    facing = grad_x + (0.8 / 0.6) * grad_y
                    energy_ref[s, lane, c : c + LIGHT, :] = energy
                    shade_ref[s, lane, c : c + LIGHT, :] = SHADE_BASE + facing * facing / (4.0 + energy)

    grad = turn(0)
    for s in range(steps):
        ready = grad
        if s + 1 < steps:
            grad = turn(s + 1)
        light(s, ready)

    def strip(i, carry):
        g = i % (groups // STRIP) * STRIP
        lane = i // (groups // STRIP)
        k = lane // halves
        m = lane % halves
        base = pl.multiple_of(g * CELL, CELL)
        zero = jnp.zeros((8, LANES), jnp.float32)
        state = [[zero, zero + 1.0, zero, zero, zero] for _ in range(2 * STRIP)]
        for s in range(steps):
            for u in range(2 * STRIP):
                if u % 2 == 0:
                    param = [param_ref[s, p, lane, pl.ds(g + u // 2, 8, stride=0), :] for p in range(6)]
                depth, trans, red, green, blue = state[u]
                at = base + 8 * u
                value = value_ref[s, k, m, pl.ds(at + SIDE, 8), :]
                energy = energy_ref[s, lane, pl.ds(at, 8), :]
                shade = shade_ref[s, lane, pl.ds(at, 8), :]
                scaled = (value - param[0]) * param[1]
                rate = jnp.exp2(param[2] - scaled * scaled)
                depth = depth - rate * energy
                after = jnp.exp2(depth)
                weight = (trans - after) * shade
                red = red + weight * param[3]
                green = green + weight * param[4]
                blue = blue + weight * param[5]
                state[u] = [depth, after, red, green, blue]
        for u in range(2 * STRIP):
            depth, trans, red, green, blue = state[u]
            at = pl.ds(base + 8 * u, 8)
            pair_a[lane, at, :] = (code(red) << 16) | code(green)
            pair_b[lane, at, :] = (code(blue) << 16) | code((1.0 - trans) * SCALE)
        return carry

    lax.fori_loop(0, groups // STRIP * count * halves, strip, 0)
    for k in range(count):
        for m in range(halves):
            if middle:
                rows = slice(m * LANES, m * LANES + LANES)
                done_a[k, rows, :] = pair_a[k * halves + m].T
                done_b[k, rows, :] = pair_b[k * halves + m].T
            else:
                row = part * (BAND * (spans[1] - spans[0])) + (BAND * spans[0] + m * LANES)
                rows = pl.ds(pl.multiple_of(row, LANES), LANES)
                turn_a[k, rows, :] = pair_a[k * halves + m].T
                turn_b[k, rows, :] = pair_b[k * halves + m].T
    if middle:
        return

    @pl.when(part == len(spans) - 1)
    def _():
        if done_a is not None:
            turn_a[:, BAND : 2 * BAND, :] = done_a[...]
            turn_b[:, BAND : 2 * BAND, :] = done_b[...]
        piece = height // out_ref.shape[0]

        def pack(d, carry):
            for u in range(8):
                e = d * 8 + u
                r = e * piece
                for k in range(count):
                    lanes = slice(LANES * k, LANES * k + LANES)
                    out_ref[e, 0:8, lanes] = turn_a[k, pl.ds(r, 8), :]
                    out_ref[e, 8:12, lanes] = turn_a[k, pl.ds(r + 8, 4), :]
                    out_ref[e, 12:16, lanes] = turn_b[k, pl.ds(r + 8, 4), :]
                    out_ref[e, 16:24, lanes] = turn_b[k, pl.ds(r, 8), :]
            return carry

        lax.fori_loop(0, out_ref.shape[0] // 8, pack, 0)


def march(tiles, spans, ranks, tables, samples, rim_rows, cells, outer=None, edges=None, done=None):
    steps, height, width = samples.shape
    first = outer is None
    middle = len(spans) == 1
    count = len(tiles)
    halves = BAND // LANES
    at = lambda n: spans[0] + n * (spans[-1] - spans[0]) // max(len(spans) - 1, 1)

    def body(*refs):
        refs = list(refs)
        if not first:
            refs[4 : 4 + count] = [refs[4 : 4 + count]]
            refs[10:10] = [None, None]
        elif middle:
            done_a, done_b, edge = refs[7:10]
            refs[7:10] = [None, edge, None, done_a, done_b]
        else:
            done_a, done_b, out, edge = refs[7:11]
            refs[7:11] = [None, edge, out, done_a, done_b]
        march_kernel(tiles, spans, (steps, height, width, steps * ranks), *refs)

    small = lambda shape: pl.BlockSpec(shape, lambda n: (0,) * len(shape))
    in_specs = [small((1, 16)), small((1, 16)), small((1, 16)), small((3, 16))]
    args = list(tables)
    if first:
        in_specs.append(pl.BlockSpec((steps, BAND, width), lambda n: (0, at(n), 0)))
        args.append(samples)
    else:
        for t in tiles:
            in_specs.append(pl.BlockSpec((steps, BAND, LANES), lambda n, t=t: (0, at(n), t)))
            args.append(samples)
    in_specs += [
        pl.BlockSpec((None, LANES, width), lambda n: (n, 0, 0)),
        pl.BlockSpec((steps, width // CELL, BAND), lambda n: (0, 0, at(n))),
    ]
    args += [rim_rows, cells]
    shape = (ranks, 2 * height // ranks, LANES * count)
    half = (count, BAND, LANES)
    if middle:
        out_shape = [jax.ShapeDtypeStruct(half, jnp.int32)] * 2
        out_specs = [small(half)] * 2
    else:
        out_shape = [jax.ShapeDtypeStruct(shape, jnp.int32)]
        out_specs = [small(shape)]
    scratch = [
        pltpu.VMEM((BAND, BAND), jnp.bfloat16),
        pltpu.VMEM((steps, RIMS, BAND), jnp.bfloat16),
        pltpu.VMEM((6, 8, LANES), jnp.float32),
        pltpu.VMEM((2, count * LANES, BAND + RIMS), jnp.bfloat16),
        pltpu.VMEM((steps, count, halves, LANES + 2 * SIDE, LANES), jnp.float32),
        pltpu.VMEM((steps, count * halves, LANES, LANES), jnp.float32),
        pltpu.VMEM((steps, count * halves, LANES, LANES), jnp.float32),
        pltpu.VMEM((steps, 6, count * halves, LANES // CELL, LANES), jnp.float32),
        pltpu.VMEM((count * halves, LANES, LANES), jnp.int32),
        pltpu.VMEM((count * halves, LANES, LANES), jnp.int32),
        pltpu.VMEM((count, height, LANES), jnp.int32),
        pltpu.VMEM((count, height, LANES), jnp.int32),
    ]
    if first:
        out_shape.append(jax.ShapeDtypeStruct((len(spans) * halves, LANES, LANES), jnp.float32))
        out_specs.append(pl.BlockSpec((halves, LANES, LANES), lambda n: (n, 0, 0)))
        scratch.append(pltpu.VMEM((width, LANES), jnp.bfloat16))
        if done is not None:
            in_specs += [small(half)] * 2
            args += done
    else:
        in_specs.append(pl.BlockSpec((2, 16, BAND), lambda n: (0, 0, n)))
        in_specs.append(pl.BlockSpec((halves, LANES, LANES), lambda n: (n, 0, 0)))
        args += [outer, edges]
    points = steps * BAND * len(spans) * LANES * count
    return pl.pallas_call(
        body,
        grid=(len(spans),),
        in_specs=in_specs,
        out_specs=out_specs,
        out_shape=out_shape,
        scratch_shapes=scratch,
        compiler_params=pltpu.CompilerParams(
            dimension_semantics=("arbitrary",), vmem_limit_bytes=56 * 1024 * 1024
        ),
        cost_estimate=pl.CostEstimate(flops=40 * points, bytes_accessed=2 * points, transcendentals=3 * points),
        name="march",
    )(*args)


def blend_kernel(tiles, order_ref, got_ref, out_ref):
    ranks = got_ref.shape[0]
    count = len(tiles)
    unroll = 8
    lower = lax.broadcasted_iota(jnp.int32, (8, LANES), 0) < 4
    zero = jnp.zeros((8, LANES), jnp.float32)
    one = zero + 1.0

    def layer(i, carry):
        carry = list(carry)
        for u in range(unroll):
            d = order_ref[i * unroll + u]
            for n in range(count):
                lanes = slice(LANES * n, LANES * n + LANES)
                red, green, blue, alpha, trans, high, low, half = carry[n]
                first = got_ref[d, 0:8, lanes]
                mixed = got_ref[d, 8:16, lanes]
                last = got_ref[d, 16:24, lanes]
                cover = decode(last & 0xFFFF) * trans
                red = red + trans * decode(lax.shift_right_logical(first, 16))
                green = green + trans * decode(first & 0xFFFF)
                blue = blue + trans * decode(lax.shift_right_logical(last, 16))
                alpha = alpha + cover
                trans = trans - cover
                level = decode(mixed & 0xFFFF)
                opaque = jnp.where(lower, pltpu.roll(level, 4, 0), level)
                high = high + half * decode(lax.shift_right_logical(mixed, 16))
                low = low + half * level
                half = half - half * opaque
                carry[n] = (red, green, blue, alpha, trans, high, low, half)
        return tuple(carry)

    start = tuple((zero, zero, zero, zero, one, zero, zero, one) for _ in range(count))
    final = lax.fori_loop(0, ranks // unroll, layer, start)
    for n in range(count):
        lanes = slice(LANES * tiles[n], LANES * tiles[n] + LANES)
        red, green, blue, alpha, _, high, low, _ = final[n]
        for r in range(8):
            for c, plane in enumerate((red, green, blue, alpha)):
                out_ref[c, r, :, lanes] = plane[r : r + 1]
        for r in range(4):
            for c, plane in enumerate((high, low)):
                out_ref[c, 8 + r, :, lanes] = plane[r : r + 1]
                out_ref[2 + c, 8 + r, :, lanes] = plane[4 + r : 5 + r]


def blend(tiles, order, got, image, width):
    ranks, rows, _ = got.shape
    whole = pl.BlockSpec(memory_space=pltpu.VMEM)
    scalars = pl.BlockSpec(memory_space=pltpu.SMEM)
    picture = jax.ShapeDtypeStruct((4, rows // 2, 1, width), jnp.float32)
    cost = pl.CostEstimate(flops=40 * got.size, bytes_accessed=4 * got.size, transcendentals=0)
    got = pltpu.with_memory_space_constraint(got, pltpu.VMEM)

    def early(place_ref, got_ref, out_ref, order_ref):
        def note(d, carry):
            order_ref[place_ref[d]] = d
            return carry

        lax.fori_loop(0, ranks, note, 0)
        blend_kernel(tiles, order_ref, got_ref, out_ref)

    def late(order_ref, got_ref, image_ref, out_ref):
        out_ref[...] = image_ref[...]
        blend_kernel(tiles, order_ref, got_ref, out_ref)

    if image is None:
        return pl.pallas_call(
            early,
            in_specs=[scalars, whole],
            out_specs=[whole, scalars],
            out_shape=[picture, jax.ShapeDtypeStruct((ranks,), jnp.int32)],
            cost_estimate=cost,
            name="blend",
        )(order, got)
    return pl.pallas_call(
        late, in_specs=[scalars, whole, whole], out_specs=whole, out_shape=picture, cost_estimate=cost, name="blend"
    )(order, got, image)


def on_device(volume, table_index, brick_position, tf_center, tf_width, tf_peak, tf_color):
    samples = volume[:, 0]
    cells = jnp.swapaxes(table_index[:, 0], 1, 2)
    steps, height, width = samples.shape
    ranks = lax.axis_size("depth")
    tables = [tf_center[None], tf_width[None], tf_peak[None], tf_color]
    tile_rank = lax.axis_index("tile")
    col_bit = tile_rank % 2
    row_bit = tile_rank // 2
    bands = height // BAND
    bare = [samples[:, n, :] for n in range(height) if 0 < n and n % BAND in (0, BAND - 1) and n < height - 1]
    pad = ((0, 0), (0, LANES - 2 * steps), (0, 0))
    send_row = jnp.where(row_bit == 0, samples[:, height - 1, :], samples[:, 0, :])
    inner_rows = jnp.pad(jnp.stack(bare[0:1] + bare[3:4], axis=1).reshape(1, 2 * steps, width), pad)
    got_row = from_partner(send_row, "tile", 1)
    *done, middle = march(CHUNKS[0], (1,), ranks, tables, samples, inner_rows, cells)
    zero_row = jnp.zeros_like(got_row)
    above = [jnp.where(row_bit == 1, got_row, zero_row), bare[1]]
    below = [bare[2], jnp.where(row_bit == 0, got_row, zero_row)]
    outer_rows = jnp.stack([jnp.stack(above, axis=1), jnp.stack(below, axis=1)], axis=0)
    outer_rows = jnp.pad(outer_rows.reshape(2, 2 * steps, width), pad)
    early, ends = march(CHUNKS[0], (0, bands - 1), ranks, tables, samples, outer_rows, cells, done=done)
    swap = functools.partial(lax.all_to_all, axis_name="depth", split_axis=0, concat_axis=0, tiled=True)
    got_early = swap(early)
    halves = BAND // LANES
    edges = jnp.concatenate([ends[:halves], middle, ends[halves:]], axis=0)
    marks = edges[:, : EDGES * steps].reshape(height // LANES, steps, EDGES, LANES)
    marks = jnp.where(col_bit == 0, marks[:, :, EDGES - 1], marks[:, :, 0])
    send_col = jnp.swapaxes(marks, 0, 1).reshape(steps, height).astype(jnp.bfloat16)
    got_col = jnp.pad(from_partner(send_col, "tile", 0).astype(jnp.float32), ((0, 16 - steps), (0, 0)))
    outer = jnp.stack([jnp.where(col_bit == 1, got_col, 0.0), jnp.where(col_bit == 0, got_col, 0.0)], axis=0)
    rows = jnp.concatenate([outer_rows[:1], inner_rows, outer_rows[1:]], axis=0)
    (late,) = march(CHUNKS[1], tuple(range(bands)), ranks, tables, samples, rows, cells, outer, edges)
    got_late = swap(late)
    image, order = blend(CHUNKS[0], brick_position, got_early, None, width)
    image = blend(CHUNKS[1], order, got_late, image, width)
    return jnp.swapaxes(image, 1, 2)


def solution(mesh):
    return jax.shard_map(
        on_device,
        mesh=mesh,
        in_specs=(
            P("depth", "tile", None, None),
            P("depth", "tile", None, None),
            P(),
            P(),
            P(),
            P(),
            P(),
        ),
        out_specs=P(None, "tile", "depth", None),
        check_vma=False,
    )
```
